128 devices in a mesh: ping: 32 (over y, x, core), rng: 4 (over z).
Axes of the slice: x: 4, y: 4, z: 4, core: 2. Of those that a mesh axis runs over, the one named last changes fastest.
Arguments:
- echoes: bfloat16 [512, 2, 32, 8192], P('ping', None, None, 'rng'), may hold values from -36 to 36, as said below
- pairing: int32 [512, 2, 8], P('ping'), may hold values from 0 to 31, as said below
- footprint: int32 [32, 48], replicated, may hold values from 0 to 511, as said below
- counts: int32 [32], replicated, may hold values from 1 to 48, 512 in all
- offsets: int32 [32, 48], replicated, may hold values from -64 to 64
- earlier: bfloat16 [32, 2, 1024, 8192], P('ping', None, None, 'rng'), may hold values from -6 to 6
Outputs:
- image: bfloat16 [32, 2, 1024, 8192], P('ping', None, None, 'rng')
The draws below stay inside these ranges and needn't reach their ends.
Inputs may be any that keep to these rules, and one draw needn't show every extreme that they name: `echoes`: the samples of a ping's pairing[p, 1] channels are partly a turned copy of ping p - 1's pairing[p, 0] channels. `pairing`: for each ping the 16 channels of its two rows are all different. `footprint`: the first counts[t] entries of row t are the pings that see tile t; the 48 entries of a row are different pings, and no aligned block of 16 pings (the pings of one ping owner, starting at a multiple of 16) holds more than 2 of them. `counts`: they sum to 512.
All inputs are finite; a program needn't handle non-finite values.
Results may differ from the reference program's by a relative error of at most 0.0053.
Values may be sent and summed in bfloat16 or wider, within the bound.
A program may use at most 192 MiB of HBM per device.

```python
import math
import jax
import jax.numpy as jnp
import numpy as np
from jax import lax

C = 32
K = 8
R = 8192
X = 1024
BAND = 64
MOST = 48
TILE_DEV = 1
PING_DEV = 16
PINGS = 512
TILES = 32
CAP = 2
N_PING = 32


def pairing_table(key):
    ping_keys = jax.random.split(jax.random.fold_in(key, 11), PINGS)
    orders = jax.vmap(lambda one_key: jax.random.permutation(one_key, C))(ping_keys)
    return jnp.stack([orders[:, :K], orders[:, K:2 * K]], axis=1).astype(jnp.int32)


def draw_pairing(key, part):
    return pairing_table(key)


def draw_echoes(key, part):
    table = pairing_table(key)
    root_key = jax.random.fold_in(key, 23)
    gain_low, gain_high = (0.3, 3.0)
    gains = jnp.exp(jax.random.uniform(jax.random.fold_in(root_key, 1), (C,), minval=math.log(gain_low), maxval=math.log(gain_high)))
    taper = 0.5 + jnp.arange(R, dtype=jnp.float32) / R
    sway = jax.random.uniform(jax.random.fold_in(root_key, 2), (PINGS,), minval=-1.0, maxval=1.0)

    def fresh_noise(one_key):
        return jnp.clip(jax.random.normal(one_key, (2, C, R)), -4.0, 4.0)
    opening = jnp.clip(fresh_noise(jax.random.fold_in(root_key, 3)), -6.0, 6.0)

    def advance(previous, inputs):
        ping_one, pair_ids, angle = inputs
        noise_now = fresh_noise(jax.random.fold_in(root_key, 100 + ping_one))
        source = previous[:, pair_ids[0], :]
        turned = angle * taper
        cos_turn = jnp.cos(turned)
        sin_turn = jnp.sin(turned)
        coherent = jnp.stack([source[0] * cos_turn - source[1] * sin_turn, source[0] * sin_turn + source[1] * cos_turn])
        current = noise_now.at[:, pair_ids[1], :].set(0.8 * coherent + 0.6 * noise_now[:, pair_ids[1], :])
        current = jnp.clip(current, -6.0, 6.0)
        return (current, current)
    steps_in = (jnp.arange(1, PINGS, dtype=jnp.int32), table[1:], sway[1:])
    closing, following = lax.scan(advance, opening, steps_in)
    whole = jnp.concatenate([opening[None], following], axis=0)
    return (whole * gains[None, None, :, None] * taper[None, None, None, :]).astype(jnp.bfloat16)


def draw_footprint(key, part):
    root_key = jax.random.fold_in(key, 37)

    def one_tile(tile_key):
        first_key, second_key = jax.random.split(tile_key)
        chosen = jax.random.permutation(first_key, N_PING * CAP)[:MOST]
        owner_ids = chosen // CAP
        rank_ids = chosen % CAP
        owner_keys = jax.random.split(second_key, N_PING)
        orders = jax.vmap(lambda one_key: jax.random.permutation(one_key, PING_DEV))(owner_keys)
        local_ids = orders[owner_ids, rank_ids]
        return (owner_ids * PING_DEV + local_ids).astype(jnp.int32)
    return jax.vmap(one_tile)(jax.random.split(root_key, TILES))


def set_ends(result, stream_key, least, largest):
    longest = result.shape.index(max(result.shape))
    spots = []
    for shift in (0, 1):
        where = [jax.random.randint(jax.random.fold_in(stream_key, axis), (), 0, length) for axis, length in enumerate(result.shape)]
        where[longest] = (where[longest] + shift) % result.shape[longest]
        spots.append(tuple(where))
    return result.at[spots[0]].set(least).at[spots[1]].set(largest)


def level_of(own_key, extent, shards, least, high):
    def one(dim, parts):
        heights = jax.random.uniform(jax.random.fold_in(jax.random.fold_in(own_key, 6), dim), (parts,), jnp.float32, least / len(shards), high / len(shards))
        return jnp.repeat(jnp.exp(heights), extent[dim] // parts).reshape((-1,) + (1,) * (len(extent) - dim - 1))

    gain = one(*shards[0])
    for cut in shards[1:]:
        gain = gain * one(*cut)
    return gain


def split_up(amount, total, reach, slope):
    loads = [(1 << 20) // math.isqrt(rank ** slope) + 1 for rank in range(2, amount + 1)]
    spare, holding = total - reach - (amount - 1), [1] * (amount - 1)
    while spare > 0:
        candidates = [i for i in range(amount - 1) if holding[i] < reach]
        pool, remaining = sum([loads[i] for i in candidates]), spare
        for i in candidates:
            extra = min(reach - holding[i], max(1, remaining * loads[i] // pool), spare)
            holding[i] = holding[i] + extra
            spare = spare - extra
    return np.array([reach] + holding)


def ragged(stream_key, number_of, total, reach, slope):
    if number_of == 2:
        one = jax.random.randint(stream_key, (), max(1, total - reach), min(reach, total - 1) + 1)
        return jnp.stack([one, total - one])
    lengths = jnp.asarray(split_up(number_of, total, reach, slope), jnp.int32)
    pairs = (number_of - 1) // 2
    giver, sink = lengths[1:1 + 2 * pairs:2], lengths[2:2 + 2 * pairs:2]
    margin = jnp.minimum(giver - 1, reach - sink)
    moved = jax.random.randint(jax.random.fold_in(stream_key, 1), (pairs,), 0, 1 << 20) % (margin + 1)
    lengths = lengths.at[1:1 + 2 * pairs:2].set(giver - moved).at[2:2 + 2 * pairs:2].set(sink + moved)
    return lengths[jax.random.permutation(jax.random.fold_in(stream_key, 2), number_of)]


def scatter_about(stream_key, dims, width, reach, cuts=(), held_as=jnp.bfloat16):
    entries = width * jax.random.normal(stream_key, dims, jnp.float32)
    if cuts:
        entries = entries * level_of(stream_key, dims, cuts, -0.22, 0.18)
    return jnp.clip(entries, -reach, reach).astype(held_as)


def setup_inputs(seed: int = 0) -> dict:
    key_list = jax.random.split(jax.random.key(seed), 7)
    echoes = draw_echoes(jax.random.fold_in(key_list[6], 71), 0)
    pairing = draw_pairing(jax.random.fold_in(key_list[6], 71), 0)
    footprint = draw_footprint(jax.random.fold_in(key_list[6], 71), 0)
    counts = ragged(key_list[3], TILES, TILES * MOST // 3, MOST, 2).astype(jnp.int32)
    offsets = set_ends(jax.random.randint(key_list[4], (TILES, MOST), -BAND, BAND + 1), jax.random.fold_in(key_list[4], 1), -BAND, BAND).astype(jnp.int32)
    earlier = scatter_about(key_list[5], (TILES, 2, X, R), 1.0, 6.0, ((0, 32), (3, 4)))
    return dict(echoes=echoes, pairing=pairing, footprint=footprint, counts=counts, offsets=offsets, earlier=earlier)


phase_modulus = 4099
small_value = 1e-06

def weight_matrix(tile_id, ping_ids, shift_ids, live_rows, tile_count):
    spacing = TILE_DEV * X // PING_DEV
    column = jnp.arange(MOST * 2 * C, dtype=jnp.int32)
    part_of = column // C % 2
    channel = column % C
    ping_cols = jnp.repeat(ping_ids, 2 * C)
    shift_cols = jnp.repeat(shift_ids, 2 * C)
    live_cols = jnp.repeat(live_rows, 2 * C)
    pixels = jnp.arange(X, dtype=jnp.int32)
    offset = tile_id * X - ping_cols * spacing - 2 * channel
    folded = jnp.remainder(pixels[:, None] + offset[None, :], phase_modulus)
    square = jnp.remainder(folded * folded, phase_modulus)
    phases = square.astype(jnp.float32) * (2.0 * math.pi / phase_modulus) + shift_cols.astype(jnp.float32)[None, :] * (math.pi / 4.0)
    scales = live_cols / jnp.sqrt(jnp.float32(C) * tile_count.astype(jnp.float32))
    cosine = jnp.cos(phases) * scales[None, :]
    sines = jnp.sin(phases) * scales[None, :]
    upper_rows = jnp.where(part_of[None, :] == 0, cosine, -sines)
    lower_rows = jnp.where(part_of[None, :] == 0, sines, cosine)
    return jnp.concatenate([upper_rows, lower_rows], axis=0).astype(jnp.bfloat16)

def reference(echoes, pairing, footprint, counts, offsets, earlier):
    front_rows = jnp.take_along_axis(echoes[:-1], pairing[1:, 0][:, None, :, None], axis=2).astype(jnp.float32)
    front_rows = jnp.concatenate([jnp.zeros((1,) + front_rows.shape[1:], jnp.float32), front_rows], axis=0)
    rear_rows = jnp.take_along_axis(echoes, pairing[:, 1][:, None, :, None], axis=2).astype(jnp.float32)
    cross_sum = lax.optimization_barrier(jnp.sum(front_rows[:, 0] * rear_rows[:, 1] - front_rows[:, 1] * rear_rows[:, 0], axis=(1, 2)))
    front_energy = lax.optimization_barrier(jnp.sum(front_rows * front_rows, axis=(1, 2, 3)))
    rear_energy = lax.optimization_barrier(jnp.sum(rear_rows * rear_rows, axis=(1, 2, 3)))
    increment = cross_sum / (jnp.sqrt(front_energy * rear_energy) + small_value)
    track_turn = jnp.cumsum(increment)
    cosine = jnp.cos(track_turn)[:, None, None]
    sines = jnp.sin(track_turn)[:, None, None]
    real_part = echoes[:, 0].astype(jnp.float32)
    imag_part = echoes[:, 1].astype(jnp.float32)
    corrected = jnp.stack([real_part * cosine + imag_part * sines, imag_part * cosine - real_part * sines], axis=1).astype(jnp.bfloat16)
    padded = jnp.pad(corrected, ((0, 0), (0, 0), (0, 0), (BAND, BAND)))

    def one_tile(tile_id):
        ping_ids = footprint[tile_id]
        shift_ids = offsets[tile_id]
        tile_count = counts[tile_id]

        def window_of(ping_one, offset_one):
            return lax.dynamic_slice_in_dim(padded[ping_one], BAND + offset_one, R, axis=2)
        window = jax.vmap(window_of)(ping_ids, shift_ids)
        live_rows = (jnp.arange(MOST, dtype=jnp.int32) < tile_count).astype(jnp.float32)
        weights = weight_matrix(tile_id, ping_ids, shift_ids, live_rows, tile_count)
        product = jnp.dot(weights.astype(jnp.float32), window.reshape(MOST * 2 * C, R).astype(jnp.float32), precision=lax.Precision.HIGHEST)
        return (earlier[tile_id].astype(jnp.float32) + product.reshape(2, X, R)).astype(jnp.bfloat16)
    return lax.map(one_tile, jnp.arange(TILES, dtype=jnp.int32))
```

```python
import functools
import math

import jax
import jax.numpy as jnp
from jax import lax
from jax.experimental import pallas as pl
from jax.experimental.pallas import tpu as pltpu
from jax.sharding import PartitionSpec as P

C = 32
X = 1024
BAND = 64
MOST = 48
PING_DEV = 16
SPACING = X // PING_DEV
CAP = 2
EDGE = 128

phase_modulus = 4099
small_value = 1e-06


def window_kernel(table, echo_ref, left_ref, right_ref, out_ref):
    slot = pl.program_id(0)
    local = table[0, slot]
    offset = table[1, slot]
    live = table[2, slot]

    @pl.when(live == 0)
    def _():
        out_ref[...] = jnp.zeros_like(out_ref)

    @pl.when(live != 0)
    def _():
        tiles = echo_ref.shape[2] // 128
        rows = echo_ref.shape[1]
        back = jnp.where(offset < 0, 1, 0)
        rem = offset + 128 * back
        turn = lax.rem(128 - rem, 128)
        lane = lax.broadcasted_iota(jnp.int32, (rows, 128), 1)
        keep = lane < 128 - rem
        left = left_ref[local].astype(jnp.float32)
        right = right_ref[local].astype(jnp.float32)
        first = echo_ref[local, :, 0:128].astype(jnp.float32)
        current = pltpu.roll(jnp.where(back == 1, left, first), turn, 1)
        for k in range(tiles):
            ahead = (
                echo_ref[local, :, 128 * (k + 1) : 128 * (k + 2)].astype(jnp.float32)
                if k + 1 < tiles
                else right
            )
            here = echo_ref[local, :, 128 * k : 128 * (k + 1)].astype(jnp.float32)
            following = pltpu.roll(jnp.where(back == 1, here, ahead), turn, 1)
            out_ref[0, :, 128 * k : 128 * (k + 1)] = jnp.where(keep, current, following).astype(
                jnp.bfloat16
            )
            current = following


def cut_windows(table, echoes, left, right):
    pings, rows, length = echoes.shape
    slots = table.shape[1]
    whole = lambda i, t: (0, 0, 0)
    return pl.pallas_call(
        window_kernel,
        out_shape=jax.ShapeDtypeStruct((slots, rows, length), jnp.bfloat16),
        grid_spec=pltpu.PrefetchScalarGridSpec(
            num_scalar_prefetch=1,
            grid=(slots,),
            in_specs=[
                pl.BlockSpec((pings, rows, length), whole),
                pl.BlockSpec((pings, rows, EDGE), whole),
                pl.BlockSpec((pings, rows, EDGE), whole),
            ],
            out_specs=pl.BlockSpec((1, rows, length), lambda i, t: (i, 0, 0)),
        ),
        cost_estimate=pl.CostEstimate(flops=0, bytes_accessed=20 << 20, transcendentals=0),
    )(table, echoes, left, right)


def weight_kernel(cos_ref, sin_ref, out_ref):
    width = cos_ref.shape[2]

    def spread(row):
        return pltpu.roll(
            jnp.broadcast_to(row, (C, width)), width - 2 * (C - 1), 1, stride=2, stride_axis=0
        )[:, :X]

    upper, lower = [], []
    for s in range(2):
        cosine = spread(cos_ref[0, s : s + 1, :])
        sine = spread(sin_ref[0, s : s + 1, :])
        upper += [cosine, -sine]
        lower += [sine, cosine]
    out_ref[0] = jnp.concatenate(upper, axis=0).T.astype(jnp.bfloat16)
    out_ref[1] = jnp.concatenate(lower, axis=0).T.astype(jnp.bfloat16)


def spread_weights(cosine, sine):
    slots, width = cosine.shape
    pairs = slots // 2
    block = pl.BlockSpec((1, 2, width), lambda i: (i, 0, 0))
    return pl.pallas_call(
        weight_kernel,
        out_shape=jax.ShapeDtypeStruct((2, X, slots * 2 * C), jnp.bfloat16),
        grid=(pairs,),
        in_specs=[block, block],
        out_specs=pl.BlockSpec((2, X, 4 * C), lambda i: (0, 0, i)),
        cost_estimate=pl.CostEstimate(flops=0, bytes_accessed=16 << 20, transcendentals=0),
    )(cosine.reshape(pairs, 2, width), sine.reshape(pairs, 2, width))


def per_device(echoes, pairing, footprint, counts, offsets, earlier):
    ping_dev = echoes.shape[0]
    block_len = echoes.shape[3]
    owners = lax.axis_size("ping")
    own_index = lax.axis_index("ping")
    rng_size = lax.axis_size("rng")
    flat = echoes.reshape(ping_dev, 2 * C, block_len)

    left = lax.ppermute(
        flat[:, :, block_len - EDGE :], "rng", [(i, i + 1) for i in range(rng_size - 1)]
    )
    right = lax.ppermute(flat[:, :, :EDGE], "rng", [(i + 1, i) for i in range(rng_size - 1)])

    positions = jnp.arange(MOST, dtype=jnp.int32)
    in_list = positions[None, :] < counts[:, None]
    owner_of = jnp.where(in_list, footprint // ping_dev, -1)
    earlier_same = jnp.sum(
        (
            (owner_of[:, None, :] == owner_of[:, :, None])
            & (positions[None, :] < positions[:, None])[None]
        ).astype(jnp.int32),
        axis=2,
    )
    slot_ids = jnp.arange(CAP, dtype=jnp.int32)

    mine = (owner_of == own_index)[:, None, :] & (earlier_same[:, None, :] == slot_ids[None, :, None])
    mine = mine.astype(jnp.int32)
    table = jnp.stack(
        [
            jnp.sum(mine * (footprint % ping_dev)[:, None, :], axis=2).reshape(-1),
            jnp.sum(mine * offsets[:, None, :], axis=2).reshape(-1),
            jnp.sum(mine, axis=2).reshape(-1),
        ]
    )
    outgoing = cut_windows(table, flat, left, right)
    received = lax.all_to_all(
        outgoing.reshape(owners, CAP, 2 * C, block_len), "ping", split_axis=0, concat_axis=0, tiled=True
    )

    channel_ids = jnp.arange(C, dtype=jnp.int32)
    front_pick = (pairing[:, 0, :, None] == channel_ids).astype(jnp.bfloat16)
    rear_pick = (pairing[:, 1, :, None] == channel_ids).astype(jnp.bfloat16)
    rear_rows = jnp.einsum("pkc,pzcr->pzkr", rear_pick, echoes, preferred_element_type=jnp.float32)
    inner_rows = jnp.einsum(
        "pkc,pzcr->pzkr", front_pick[1:], echoes[:-1], preferred_element_type=jnp.float32
    )
    last_ping = lax.ppermute(echoes[-1], "ping", [(i, i + 1) for i in range(owners - 1)])
    lead_rows = jnp.einsum("kc,zcr->zkr", front_pick[0], last_ping, preferred_element_type=jnp.float32)
    front_rows = jnp.concatenate([lead_rows[None], inner_rows], axis=0)
    cross_sum = jnp.sum(
        front_rows[:, 0] * rear_rows[:, 1] - front_rows[:, 1] * rear_rows[:, 0], axis=(1, 2)
    )
    front_energy = jnp.sum(front_rows * front_rows, axis=(1, 2, 3))
    rear_energy = jnp.sum(rear_rows * rear_rows, axis=(1, 2, 3))
    sums = lax.all_gather(jnp.stack([cross_sum, front_energy, rear_energy]), ("ping", "rng"))
    sums = jnp.sum(sums.reshape(owners, rng_size, 3, ping_dev), axis=1)
    increment = sums[:, 0] / (jnp.sqrt(sums[:, 1] * sums[:, 2]) + small_value)
    increment = increment.reshape(-1)
    every = jnp.arange(owners * ping_dev, dtype=jnp.int32)
    track_turn = jnp.sum(
        jnp.where(every[None, :] <= every[:, None], increment[None, :], 0.0), axis=1
    )

    tile_id = own_index
    pick_owner = jnp.arange(owners, dtype=jnp.int32)
    own_owner = lax.dynamic_index_in_dim(owner_of, tile_id, 0, keepdims=False)
    own_rank = lax.dynamic_index_in_dim(earlier_same, tile_id, 0, keepdims=False)
    own_foot = lax.dynamic_index_in_dim(footprint, tile_id, 0, keepdims=False)
    own_offset = lax.dynamic_index_in_dim(offsets, tile_id, 0, keepdims=False)
    own_count = lax.dynamic_index_in_dim(counts, tile_id, 0, keepdims=False)
    held = (own_owner[None, None, :] == pick_owner[:, None, None]) & (
        own_rank[None, None, :] == slot_ids[None, :, None]
    )
    held = held.astype(jnp.int32).reshape(owners * CAP, MOST)
    live = jnp.sum(held, axis=1).astype(jnp.float32)
    ping_ids = jnp.sum(held * own_foot[None, :], axis=1)
    shift_ids = jnp.sum(held * own_offset[None, :], axis=1)
    turn = jnp.sum(jnp.where(every[None, :] == ping_ids[:, None], track_turn[None, :], 0.0), axis=1)

    width = X + 128
    start = tile_id * X - ping_ids * SPACING - 2 * (C - 1)
    along = jnp.arange(width, dtype=jnp.int32)
    folded = jnp.remainder(start[:, None] + along[None, :], phase_modulus)
    square = jnp.remainder(folded * folded, phase_modulus)
    phases = square.astype(jnp.float32) * (2.0 * math.pi / phase_modulus) + (
        shift_ids.astype(jnp.float32) * (math.pi / 4.0) - turn
    )[:, None]
    scales = live / jnp.sqrt(jnp.float32(C) * own_count.astype(jnp.float32))
    weights = spread_weights(jnp.cos(phases) * scales[:, None], jnp.sin(phases) * scales[:, None])

    contribution = jnp.dot(
        weights.reshape(2 * X, -1),
        received.reshape(-1, block_len),
        preferred_element_type=jnp.float32,
    ).reshape(1, 2, X, block_len)
    return (earlier.astype(jnp.float32) + contribution).astype(jnp.bfloat16)


def solution(mesh):
    return jax.shard_map(
        per_device,
        mesh=mesh,
        in_specs=(
            P("ping", None, None, "rng"),
            P("ping", None, None),
            P(),
            P(),
            P(),
            P("ping", None, None, "rng"),
        ),
        out_specs=P("ping", None, None, "rng"),
        check_vma=False,
    )
```

```python
import functools
import math

import jax
import jax.numpy as jnp
from jax import lax
from jax.experimental import pallas as pl
from jax.experimental.pallas import tpu as pltpu
from jax.sharding import PartitionSpec as P

C = 32
X = 1024
MOST = 48
PING_DEV = 16
SPACING = X // PING_DEV
SIDE = 4
CORES = 2
HOLD = 8
MESH = pl.DeviceIdType.MESH
ANY = pl.BlockSpec(memory_space=pl.ANY)
IN_VMEM = pl.BlockSpec(memory_space=pltpu.VMEM)

phase_modulus = 4099
small_value = 1e-06


def place(index):
    return index // (SIDE * CORES), (index // CORES) % SIDE, index % CORES


def device(y, x, c):
    return (((y + SIDE) % SIDE) * SIDE + (x + SIDE) % SIDE) * CORES + (c + CORES) % CORES


def gather_kernel(
    rng_size,
    echo_ref,
    front_ref,
    rear_ref,
    row_ref,
    column_ref,
    row_edge_ref,
    column_edge_ref,
    sums_ref,
    held,
    beside,
    edges,
    partial,
    total,
    local_sem,
    send_sem,
    recv_sem,
    sum_send,
    sum_recv,
):
    me = lax.axis_index("ping")
    level = lax.axis_index("rng")
    y, x, c = place(me)
    owners = SIDE * SIDE * CORES
    pings, half = PING_DEV, PING_DEV // 2
    length = echo_ref.shape[3]

    barrier = pltpu.get_barrier_semaphore()
    for step in range(1, owners):
        pl.semaphore_signal(
            barrier, inc=1, device_id={"ping": (me + step) % owners}, device_id_type=MESH
        )
    for step in range(1, rng_size):
        pl.semaphore_signal(
            barrier, inc=1, device_id={"rng": (level + step) % rng_size}, device_id_type=MESH
        )
    own = pltpu.make_async_copy(echo_ref, held.at[pl.ds(1, pings)], local_sem.at[0])
    own.start()
    pl.semaphore_wait(barrier, owners + rng_size - 2)

    started = []

    def send(src, dst, target):
        i = len(started)
        copy = pltpu.make_async_remote_copy(
            src_ref=src,
            dst_ref=dst,
            send_sem=send_sem.at[i],
            recv_sem=recv_sem.at[i],
            device_id=target,
            device_id_type=MESH,
        )
        copy.start()
        started.append(copy)
        return copy

    up, down = {"rng": (level + 1) % rng_size}, {"rng": (level + rng_size - 1) % rng_size}
    ahead = {"ping": device(y, x + 1, c)}
    behind = {"ping": device(y, x - 1, c)}
    above = {"ping": device(y + 1, x, c)}
    below = {"ping": device(y - 1, x, c)}
    lead = send(echo_ref.at[pings - 1], held.at[0], {"ping": (me + 1) % owners})
    from_low = send(echo_ref.at[:, :, :, pl.ds(length - 128, 128)], beside.at[0], up)
    from_high = send(echo_ref.at[:, :, :, pl.ds(0, 128)], beside.at[1], down)
    low, high = pl.ds(0, half), pl.ds(half, half)
    row_forward = [
        send(echo_ref.at[part, 0], row_ref.at[2, part], ahead) for part in (low,)
    ]
    row_backward = [send(echo_ref.at[high, 0], row_ref.at[0, high], behind)]
    column_forward = [send(echo_ref.at[low, 1], column_ref.at[2, low], above)]
    column_backward = [send(echo_ref.at[high, 1], column_ref.at[0, high], below)]
    row_forward.append(send(echo_ref.at[high, 0], row_ref.at[2, high], ahead))
    row_backward.append(send(echo_ref.at[low, 0], row_ref.at[0, low], behind))
    column_forward.append(send(echo_ref.at[high, 1], column_ref.at[2, high], above))
    column_backward.append(send(echo_ref.at[low, 1], column_ref.at[0, low], below))

    from_low.wait_recv()
    from_high.wait_recv()
    lane = lax.broadcasted_iota(jnp.int32, (C, 128), 1)
    use_low = level > 0
    use_high = level < rng_size - 1

    def merge(p, carry):
        for part in range(2):
            low_edge = beside[0, p, part].astype(jnp.float32)
            high_edge = beside[1, p, part].astype(jnp.float32)
            merged = jnp.where(
                lane < 64,
                jnp.where(use_high, high_edge, 0.0),
                jnp.where(use_low, low_edge, 0.0),
            )
            edges[part, p] = merged.astype(jnp.bfloat16)
        return carry

    lax.fori_loop(0, pings, merge, 0)
    row_edges = [
        send(edges.at[0], row_edge_ref.at[3], ahead),
        send(edges.at[0], row_edge_ref.at[1], behind),
    ]
    column_edges = [
        send(edges.at[1], column_edge_ref.at[3], above),
        send(edges.at[1], column_edge_ref.at[1], below),
    ]
    own_edges = [
        pltpu.make_async_copy(edges.at[0], row_edge_ref.at[0], local_sem.at[1]),
        pltpu.make_async_copy(edges.at[1], column_edge_ref.at[0], local_sem.at[2]),
    ]
    for copy in own_edges:
        copy.start()

    own.wait()
    lead.wait_recv()
    first = (me > 0).astype(jnp.float32)
    place_lane = lax.broadcasted_iota(jnp.int32, (8, 128), 1)

    def fold(value):
        out = value[:, 0:128]
        for k in range(1, length // 128):
            out = out + value[:, 128 * k : 128 * (k + 1)]
        out = jnp.sum(out, axis=0, keepdims=True)
        return jnp.sum(out, axis=1, keepdims=True)

    def correlate(p, acc):
        front, rear = front_ref[p], rear_ref[p]
        scale = jnp.where(p == 0, first, 1.0)
        dot = functools.partial(jnp.dot, preferred_element_type=jnp.float32)
        front_real = dot(front, held[p, 0]) * scale
        front_imag = dot(front, held[p, 1]) * scale
        rear_real = dot(rear, held[p + 1, 0])
        rear_imag = dot(rear, held[p + 1, 1])
        acc = jnp.where(place_lane == p, fold(front_real * rear_imag - front_imag * rear_real), acc)
        acc = jnp.where(
            place_lane == p + pings, fold(front_real * front_real + front_imag * front_imag), acc
        )
        return jnp.where(
            place_lane == p + 2 * pings, fold(rear_real * rear_real + rear_imag * rear_imag), acc
        )

    mine = lax.fori_loop(0, pings, correlate, jnp.zeros((8, 128), jnp.float32))
    partial[0] = mine
    across = []
    for step in range(1, rng_size):
        across.append(
            pltpu.make_async_remote_copy(
                src_ref=partial.at[0],
                dst_ref=partial.at[step],
                send_sem=sum_send.at[owners + step],
                recv_sem=sum_recv.at[owners + step],
                device_id={"rng": (level + step) % rng_size},
                device_id_type=MESH,
            )
        )
        across[-1].start()
    for copy in across:
        copy.wait_recv()
    whole = mine
    for step in range(1, rng_size):
        whole = whole + partial[step]
    total[...] = whole
    own_total = pltpu.make_async_copy(total, sums_ref.at[me], local_sem.at[3])
    own_total.start()
    spread = []
    for step in range(1, owners):
        spread.append(
            pltpu.make_async_remote_copy(
                src_ref=total,
                dst_ref=sums_ref.at[me],
                send_sem=sum_send.at[step],
                recv_sem=sum_recv.at[step],
                device_id={"ping": (me + step) % owners},
                device_id_type=MESH,
            )
        )
        spread[-1].start()

    relays = []
    row_forward[0].wait_recv()
    relays.append(send(row_ref.at[2, low], row_ref.at[1, low], ahead))
    row_backward[0].wait_recv()
    relays.append(send(row_ref.at[0, high], row_ref.at[1, high], behind))
    column_forward[0].wait_recv()
    relays.append(send(column_ref.at[2, low], column_ref.at[1, low], above))
    column_backward[0].wait_recv()
    relays.append(send(column_ref.at[0, high], column_ref.at[1, high], below))
    for copies, out, forth, back in (
        (row_edges, row_edge_ref, ahead, behind),
        (column_edges, column_edge_ref, above, below),
    ):
        copies[0].wait_recv()
        relays.append(send(out.at[3, low], out.at[2, low], forth))
        copies[1].wait_recv()
        relays.append(send(out.at[1, high], out.at[2, high], back))
    for copies in (row_forward, row_backward, column_forward, column_backward):
        copies[1].wait_recv()
    for copy in relays:
        copy.wait_recv()
    for copy in spread:
        copy.wait_recv()
    for copy in started + spread + across:
        copy.wait_send()
    for copy in own_edges:
        copy.wait()
    own_total.wait()


def gather_pings(echoes, front_pick, rear_pick, rng_size):
    pings, parts, channels, length = echoes.shape
    owners = SIDE * SIDE * CORES
    block = (pings, channels, length)
    edge = (pings, channels, 128)
    bf16 = jnp.bfloat16
    copies = 3 + 8 + 4 + 8
    return pl.pallas_call(
        functools.partial(gather_kernel, rng_size),
        out_shape=(
            jax.ShapeDtypeStruct((SIDE - 1,) + block, bf16),
            jax.ShapeDtypeStruct((SIDE - 1,) + block, bf16),
            jax.ShapeDtypeStruct((SIDE,) + edge, bf16),
            jax.ShapeDtypeStruct((SIDE,) + edge, bf16),
            jax.ShapeDtypeStruct((owners, 8, 128), jnp.float32),
        ),
        in_specs=[ANY, IN_VMEM, IN_VMEM],
        out_specs=(ANY,) * 5,
        scratch_shapes=[
            pltpu.VMEM((pings + 1, parts, channels, length), bf16),
            pltpu.VMEM((2, pings, parts, channels, 128), bf16),
            pltpu.VMEM((parts,) + edge, bf16),
            pltpu.VMEM((rng_size, 8, 128), jnp.float32),
            pltpu.VMEM((8, 128), jnp.float32),
            pltpu.SemaphoreType.DMA((4,)),
            pltpu.SemaphoreType.DMA((copies,)),
            pltpu.SemaphoreType.DMA((copies,)),
            pltpu.SemaphoreType.DMA((owners + rng_size,)),
            pltpu.SemaphoreType.DMA((owners + rng_size,)),
        ],
        compiler_params=pltpu.CompilerParams(collective_id=0, has_side_effects=True),
        name="gather_pings",
    )(echoes, front_pick, rear_pick)


def window_kernel(table, echo_ref, row_ref, column_ref, row_edge_ref, column_edge_ref, out_ref, held, edge, sem):
    step = pl.program_id(0)
    pings, length = PING_DEV, held.shape[3]
    tiles = length // 128

    @pl.when(step == 0)
    def _():
        copies = []
        for part, gathered, gathered_edge in ((0, row_ref, row_edge_ref), (1, column_ref, column_edge_ref)):
            copies.append(pltpu.make_async_copy(echo_ref.at[:, part], held.at[part, 0:pings], sem.at[part, 0]))
            for d in range(1, SIDE):
                copies.append(
                    pltpu.make_async_copy(
                        gathered.at[d - 1], held.at[part, pings * d : pings * (d + 1)], sem.at[part, d]
                    )
                )
            for d in range(SIDE):
                copies.append(
                    pltpu.make_async_copy(
                        gathered_edge.at[d], edge.at[part, pings * d : pings * (d + 1)], sem.at[part, SIDE + d]
                    )
                )
        for copy in copies:
            copy.start()
        for copy in copies:
            copy.wait()

    part = step // HOLD
    lane = lax.broadcasted_iota(jnp.int32, (C, 128), 1)

    def one_slot(s, carry):
        local = table[0, step * HOLD + s]
        offset = table[1, step * HOLD + s]
        live = table[2, step * HOLD + s]

        @pl.when(live != 0)
        def _():
            back = offset < 0
            rem = jnp.where(back, offset + 128, offset)
            turn = lax.rem(128 - rem, 128)
            keep = lane < 128 - rem
            outside = edge[part, local].astype(jnp.float32)
            here = held[part, local, :, 0:128].astype(jnp.float32)
            current = pltpu.roll(jnp.where(back, outside, here), turn, 1)
            for k in range(tiles):
                ahead = (
                    held[part, local, :, 128 * (k + 1) : 128 * (k + 2)].astype(jnp.float32)
                    if k + 1 < tiles
                    else outside
                )
                following = pltpu.roll(jnp.where(back, here, ahead), turn, 1)
                out_ref[0, s, :, 128 * k : 128 * (k + 1)] = jnp.where(keep, current, following).astype(
                    jnp.bfloat16
                )
                current, here = following, ahead

        return carry

    lax.fori_loop(0, HOLD, one_slot, 0)


def cut_windows(table, echoes, row, column, row_edge, column_edge):
    pings, parts, channels, length = echoes.shape
    groups = 2 * HOLD
    return pl.pallas_call(
        window_kernel,
        out_shape=jax.ShapeDtypeStruct((groups, HOLD, channels, length), jnp.bfloat16),
        grid_spec=pltpu.PrefetchScalarGridSpec(
            num_scalar_prefetch=1,
            grid=(groups,),
            in_specs=[ANY] * 5,
            out_specs=pl.BlockSpec((1, HOLD, channels, length), lambda i, t: (i, 0, 0, 0)),
            scratch_shapes=[
                pltpu.VMEM((parts, SIDE * pings, channels, length), jnp.bfloat16),
                pltpu.VMEM((parts, SIDE * pings, channels, 128), jnp.bfloat16),
                pltpu.SemaphoreType.DMA((parts, 2 * SIDE)),
            ],
        ),
        name="cut_windows",
    )(table, echoes, row, column, row_edge, column_edge)


def exchange_kernel(slots_ref, received_ref, local_sem, send_sem, recv_sem):
    me = lax.axis_index("ping")
    y, x, c = place(me)
    targets = []
    for part in range(2):
        for k in range(1, HOLD):
            d, dc = k // CORES, k % CORES
            to = device(y + d, x, c + dc) if part == 0 else device(y, x + d, c + dc)
            targets.append((part * HOLD + k, to))
    barrier = pltpu.get_barrier_semaphore()
    for _, to in targets:
        pl.semaphore_signal(barrier, inc=1, device_id={"ping": to}, device_id_type=MESH)
    own = [
        pltpu.make_async_copy(
            slots_ref.at[part * HOLD], received_ref.at[part * HOLD], local_sem.at[part]
        )
        for part in range(2)
    ]
    for copy in own:
        copy.start()
    pl.semaphore_wait(barrier, len(targets))
    copies = []
    order = sorted(range(len(targets)), key=lambda i: (targets[i][0] % HOLD, targets[i][0]))
    for i in order:
        group, to = targets[i]
        copies.append(
            pltpu.make_async_remote_copy(
                src_ref=slots_ref.at[group],
                dst_ref=received_ref.at[group],
                send_sem=send_sem.at[i],
                recv_sem=recv_sem.at[i],
                device_id={"ping": to},
                device_id_type=MESH,
            )
        )
        copies[-1].start()
    for copy in copies:
        copy.wait()
    for copy in own:
        copy.wait()


def exchange(slots):
    count = 2 * (HOLD - 1)
    return pl.pallas_call(
        exchange_kernel,
        out_shape=jax.ShapeDtypeStruct(slots.shape, slots.dtype),
        in_specs=[ANY],
        out_specs=ANY,
        scratch_shapes=[
            pltpu.SemaphoreType.DMA((2,)),
            pltpu.SemaphoreType.DMA((count,)),
            pltpu.SemaphoreType.DMA((count,)),
        ],
        compiler_params=pltpu.CompilerParams(collective_id=1, has_side_effects=True),
        name="exchange",
    )(slots)


def weight_kernel(cos_ref, sin_ref, out_ref):
    width = cos_ref.shape[2]

    def spread(row):
        return pltpu.roll(
            jnp.broadcast_to(row, (C, width)), width - 2 * (C - 1), 1, stride=2, stride_axis=0
        )[:, :X]

    upper, lower = [], []
    for s in range(2):
        cosine = spread(cos_ref[0, s : s + 1, :])
        sine = spread(sin_ref[0, s : s + 1, :])
        upper += [cosine, -sine]
        lower += [sine, cosine]
    out_ref[0] = jnp.concatenate(upper, axis=0).T.astype(jnp.bfloat16)
    out_ref[1] = jnp.concatenate(lower, axis=0).T.astype(jnp.bfloat16)


def spread_weights(cosine, sine):
    slots, width = cosine.shape
    pairs = slots // 2
    block = pl.BlockSpec((1, 2, width), lambda i: (i, 0, 0))
    return pl.pallas_call(
        weight_kernel,
        out_shape=jax.ShapeDtypeStruct((2, X, slots * 2 * C), jnp.bfloat16),
        grid=(pairs,),
        in_specs=[block, block],
        out_specs=pl.BlockSpec((2, X, 4 * C), lambda i: (0, 0, i)),
        name="spread_weights",
    )(cosine.reshape(pairs, 2, width), sine.reshape(pairs, 2, width))


def focus_kernel(table, weight_ref, real_ref, imag_ref, earlier_ref, out_ref, stacked):
    rows = 256

    def fill(j, carry):
        for part, source in ((0, real_ref), (1, imag_ref)):
            slot = table[part, j]
            at = pl.multiple_of(j * 2 * C + part * C, C)
            stacked[pl.ds(at, C), :] = source[slot // HOLD, slot % HOLD]
        return carry

    lax.fori_loop(0, MOST, fill, 0)

    def multiply(i, carry):
        at = pl.ds(pl.multiple_of(i * rows, rows), rows)
        product = jnp.dot(weight_ref[at, :], stacked[...], preferred_element_type=jnp.float32)
        out_ref[at, :] = (earlier_ref[at, :].astype(jnp.float32) + product).astype(jnp.bfloat16)
        return carry

    lax.fori_loop(0, 2 * X // rows, multiply, 0)


def focus(table, weights, received, earlier):
    groups, hold, channels, length = received.shape
    wide = 512
    return pl.pallas_call(
        focus_kernel,
        out_shape=jax.ShapeDtypeStruct((2 * X, length), jnp.bfloat16),
        grid_spec=pltpu.PrefetchScalarGridSpec(
            num_scalar_prefetch=1,
            grid=(length // wide,),
            in_specs=[
                pl.BlockSpec(weights.shape, lambda n, t: (0, 0), pipeline_mode=pl.Buffered(1)),
                pl.BlockSpec((HOLD, hold, channels, wide), lambda n, t: (0, 0, 0, n)),
                pl.BlockSpec((HOLD, hold, channels, wide), lambda n, t: (1, 0, 0, n)),
                pl.BlockSpec((2 * X, wide), lambda n, t: (0, n)),
            ],
            out_specs=pl.BlockSpec((2 * X, wide), lambda n, t: (0, n)),
            scratch_shapes=[pltpu.VMEM((MOST * 2 * C, wide), jnp.bfloat16)],
        ),
        name="focus",
    )(table, weights, received, received, earlier)


def rank_in(groups, positions):
    same = (groups[:, None, :] == groups[:, :, None]) & (positions[None, :] < positions[:, None])[None]
    return jnp.sum(same.astype(jnp.int32), axis=2)


def per_device(echoes, pairing, footprint, counts, offsets, earlier):
    block_len = echoes.shape[3]
    owners = lax.axis_size("ping")
    rng_size = lax.axis_size("rng")
    me = lax.axis_index("ping")
    y, x, c = place(me)

    channel_ids = jnp.arange(C, dtype=jnp.int32)
    front_pick = (pairing[:, 0, :, None] == channel_ids).astype(jnp.bfloat16)
    rear_pick = (pairing[:, 1, :, None] == channel_ids).astype(jnp.bfloat16)
    row, column, row_edge, column_edge, sums = gather_pings(echoes, front_pick, rear_pick, rng_size)

    steps = jnp.arange(HOLD, dtype=jnp.int32)
    tiles = jnp.concatenate(
        [
            device(y + steps // CORES, x, c + steps % CORES),
            device(y, x + steps // CORES, c + steps % CORES),
        ]
    )
    all_tiles = jnp.arange(owners, dtype=jnp.int32)
    chosen = (tiles[:, None] == all_tiles[None, :]).astype(jnp.int32)
    positions = jnp.arange(MOST, dtype=jnp.int32)
    foot = jnp.sum(chosen[:, :, None] * footprint[None], axis=1)
    shift = jnp.sum(chosen[:, :, None] * offsets[None], axis=1)
    count = jnp.sum(chosen * counts[None, :], axis=1)
    listed = positions[None, :] < count[:, None]
    oy, ox, oc = place(foot // PING_DEV)
    by_row = steps[:, None] >= 0
    by_row = jnp.concatenate([by_row, ~by_row], axis=0)
    group = jnp.where(listed, jnp.where(by_row, oy, ox) * CORES + oc, -1)
    rank = rank_in(group, positions)
    here = group == jnp.where(by_row, y, x) * CORES + c
    distance = jnp.where(by_row, ox - x + SIDE, oy - y + SIDE) % SIDE
    source = distance * PING_DEV + foot % PING_DEV
    fits = (here[:, None, :] & (rank[:, None, :] == steps[None, :, None])).astype(jnp.int32)
    table = jnp.stack(
        [
            jnp.sum(fits * source[:, None, :], axis=2).reshape(-1),
            jnp.sum(fits * shift[:, None, :], axis=2).reshape(-1),
            jnp.sum(fits, axis=2).reshape(-1),
        ]
    )
    slots = cut_windows(table, echoes, row, column, row_edge, column_edge)
    received = exchange(slots)

    own_group = jnp.stack([group[0], group[HOLD]])
    own_rank = jnp.stack([rank[0], rank[HOLD]])
    own_place = jnp.stack([y, x])[:, None]
    own_distance = (own_place - own_group // CORES + SIDE) % SIDE
    own_core = (c - own_group % CORES + CORES) % CORES
    arrival = jnp.where(listed[0:1], (own_distance * CORES + own_core) * HOLD + own_rank, -1)
    arrival = jnp.where(listed[0:1], arrival, arrival[:, 0:1])

    sums = sums[:, 0, :]
    cross, front, rear = (sums[:, k * PING_DEV : (k + 1) * PING_DEV] for k in range(3))
    increment = (cross / (jnp.sqrt(front * rear) + small_value)).reshape(-1)
    every = jnp.arange(owners * PING_DEV, dtype=jnp.int32)
    track_turn = jnp.sum(jnp.where(every[None, :] <= every[:, None], increment[None, :], 0.0), axis=1)
    turn = jnp.sum(jnp.where(every[None, :] == foot[0][:, None], track_turn[None, :], 0.0), axis=1)

    width = X + 128
    start = me * X - foot[0] * SPACING - 2 * (C - 1)
    along = jnp.arange(width, dtype=jnp.int32)
    folded = jnp.remainder(start[:, None] + along[None, :], phase_modulus)
    square = jnp.remainder(folded * folded, phase_modulus)
    phases = square.astype(jnp.float32) * (2.0 * math.pi / phase_modulus) + (
        shift[0].astype(jnp.float32) * (math.pi / 4.0) - turn
    )[:, None]
    scales = listed[0].astype(jnp.float32) / jnp.sqrt(jnp.float32(C) * count[0].astype(jnp.float32))
    weights = spread_weights(jnp.cos(phases) * scales[:, None], jnp.sin(phases) * scales[:, None])

    image = focus(arrival, weights.reshape(2 * X, -1), received, earlier.reshape(2 * X, block_len))
    return image.reshape(earlier.shape)


def solution(mesh):
    return jax.shard_map(
        per_device,
        mesh=mesh,
        in_specs=(
            P("ping", None, None, "rng"),
            P("ping", None, None),
            P(),
            P(),
            P(),
            P("ping", None, None, "rng"),
        ),
        out_specs=P("ping", None, None, "rng"),
        check_vma=False,
    )
```

```python
import functools
import math

import jax
import jax.numpy as jnp
from jax import lax
from jax.experimental import pallas as pl
from jax.experimental.pallas import tpu as pltpu
from jax.sharding import PartitionSpec as P

C = 32
X = 1024
MOST = 48
PING_DEV = 16
SPACING = X // PING_DEV
SIDE = 4
CORES = 2
HOLD = 8
MESH = pl.DeviceIdType.MESH
ANY = pl.BlockSpec(memory_space=pl.ANY)
IN_VMEM = pl.BlockSpec(memory_space=pltpu.VMEM)

phase_modulus = 4099
small_value = 1e-06


def place(index):
    return index // (SIDE * CORES), (index // CORES) % SIDE, index % CORES


def device(y, x, c):
    return (((y + SIDE) % SIDE) * SIDE + (x + SIDE) % SIDE) * CORES + (c + CORES) % CORES


def gather_kernel(
    rng_size,
    echo_ref,
    front_ref,
    rear_ref,
    row_ref,
    column_ref,
    row_edge_ref,
    column_edge_ref,
    sums_ref,
    held,
    beside,
    edges,
    partial,
    total,
    local_sem,
    send_sem,
    recv_sem,
    sum_send,
    sum_recv,
):
    me = lax.axis_index("ping")
    level = lax.axis_index("rng")
    y, x, c = place(me)
    owners = SIDE * SIDE * CORES
    pings, half = PING_DEV, PING_DEV // 2
    length = echo_ref.shape[3]

    barrier = pltpu.get_barrier_semaphore()
    for step in range(1, owners):
        pl.semaphore_signal(
            barrier, inc=1, device_id={"ping": (me + step) % owners}, device_id_type=MESH
        )
    for step in range(1, rng_size):
        pl.semaphore_signal(
            barrier, inc=1, device_id={"rng": (level + step) % rng_size}, device_id_type=MESH
        )
    own = pltpu.make_async_copy(echo_ref, held.at[pl.ds(1, pings)], local_sem.at[0])
    own.start()
    pl.semaphore_wait(barrier, owners + rng_size - 2)

    started = []

    def send(src, dst, target):
        i = len(started)
        copy = pltpu.make_async_remote_copy(
            src_ref=src,
            dst_ref=dst,
            send_sem=send_sem.at[i],
            recv_sem=recv_sem.at[i],
            device_id=target,
            device_id_type=MESH,
        )
        copy.start()
        started.append(copy)
        return copy

    up, down = {"rng": (level + 1) % rng_size}, {"rng": (level + rng_size - 1) % rng_size}
    ahead = {"ping": device(y, x + 1, c)}
    behind = {"ping": device(y, x - 1, c)}
    above = {"ping": device(y + 1, x, c)}
    below = {"ping": device(y - 1, x, c)}
    lead = send(echo_ref.at[pings - 1], held.at[0], {"ping": (me + 1) % owners})
    from_low = send(echo_ref.at[:, :, :, pl.ds(length - 128, 128)], beside.at[0], up)
    from_high = send(echo_ref.at[:, :, :, pl.ds(0, 128)], beside.at[1], down)
    low, high = pl.ds(0, half), pl.ds(half, half)
    row_forward = [
        send(echo_ref.at[part, 0], row_ref.at[2, part], ahead) for part in (low,)
    ]
    row_backward = [send(echo_ref.at[high, 0], row_ref.at[0, high], behind)]
    column_forward = [send(echo_ref.at[low, 1], column_ref.at[2, low], above)]
    column_backward = [send(echo_ref.at[high, 1], column_ref.at[0, high], below)]
    row_forward.append(send(echo_ref.at[high, 0], row_ref.at[2, high], ahead))
    row_backward.append(send(echo_ref.at[low, 0], row_ref.at[0, low], behind))
    column_forward.append(send(echo_ref.at[high, 1], column_ref.at[2, high], above))
    column_backward.append(send(echo_ref.at[low, 1], column_ref.at[0, low], below))

    from_low.wait_recv()
    from_high.wait_recv()
    lane = lax.broadcasted_iota(jnp.int32, (C, 128), 1)
    use_low = level > 0
    use_high = level < rng_size - 1

    def merge(p, carry):
        for part in range(2):
            low_edge = beside[0, p, part].astype(jnp.float32)
            high_edge = beside[1, p, part].astype(jnp.float32)
            merged = jnp.where(
                lane < 64,
                jnp.where(use_high, high_edge, 0.0),
                jnp.where(use_low, low_edge, 0.0),
            )
            edges[part, p] = merged.astype(jnp.bfloat16)
        return carry

    lax.fori_loop(0, pings, merge, 0)
    row_edges = [
        send(edges.at[0], row_edge_ref.at[3], ahead),
        send(edges.at[0], row_edge_ref.at[1], behind),
    ]
    column_edges = [
        send(edges.at[1], column_edge_ref.at[3], above),
        send(edges.at[1], column_edge_ref.at[1], below),
    ]
    own_edges = [
        pltpu.make_async_copy(edges.at[0], row_edge_ref.at[0], local_sem.at[1]),
        pltpu.make_async_copy(edges.at[1], column_edge_ref.at[0], local_sem.at[2]),
    ]
    for copy in own_edges:
        copy.start()

    own.wait()
    lead.wait_recv()
    first = (me > 0).astype(jnp.float32)
    place_lane = lax.broadcasted_iota(jnp.int32, (8, 128), 1)

    def fold(value):
        out = value[:, 0:128]
        for k in range(1, length // 128):
            out = out + value[:, 128 * k : 128 * (k + 1)]
        out = jnp.sum(out, axis=0, keepdims=True)
        return jnp.sum(out, axis=1, keepdims=True)

    def correlate(p, acc):
        front, rear = front_ref[p], rear_ref[p]
        scale = jnp.where(p == 0, first, 1.0)
        dot = functools.partial(jnp.dot, preferred_element_type=jnp.float32)
        front_real = dot(front, held[p, 0]) * scale
        front_imag = dot(front, held[p, 1]) * scale
        rear_real = dot(rear, held[p + 1, 0])
        rear_imag = dot(rear, held[p + 1, 1])
        acc = jnp.where(place_lane == p, fold(front_real * rear_imag - front_imag * rear_real), acc)
        acc = jnp.where(
            place_lane == p + pings, fold(front_real * front_real + front_imag * front_imag), acc
        )
        return jnp.where(
            place_lane == p + 2 * pings, fold(rear_real * rear_real + rear_imag * rear_imag), acc
        )

    mine = lax.fori_loop(0, pings, correlate, jnp.zeros((8, 128), jnp.float32))
    partial[0] = mine
    across = []
    for step in range(1, rng_size):
        across.append(
            pltpu.make_async_remote_copy(
                src_ref=partial.at[0],
                dst_ref=partial.at[step],
                send_sem=sum_send.at[owners + step],
                recv_sem=sum_recv.at[owners + step],
                device_id={"rng": (level + step) % rng_size},
                device_id_type=MESH,
            )
        )
        across[-1].start()
    for copy in across:
        copy.wait_recv()
    whole = mine
    for step in range(1, rng_size):
        whole = whole + partial[step]
    total[...] = whole
    own_total = pltpu.make_async_copy(total, sums_ref.at[me], local_sem.at[3])
    own_total.start()
    spread = []
    for step in range(1, owners):
        spread.append(
            pltpu.make_async_remote_copy(
                src_ref=total,
                dst_ref=sums_ref.at[me],
                send_sem=sum_send.at[step],
                recv_sem=sum_recv.at[step],
                device_id={"ping": (me + step) % owners},
                device_id_type=MESH,
            )
        )
        spread[-1].start()

    relays = []
    row_forward[0].wait_recv()
    relays.append(send(row_ref.at[2, low], row_ref.at[1, low], ahead))
    row_backward[0].wait_recv()
    relays.append(send(row_ref.at[0, high], row_ref.at[1, high], behind))
    column_forward[0].wait_recv()
    relays.append(send(column_ref.at[2, low], column_ref.at[1, low], above))
    column_backward[0].wait_recv()
    relays.append(send(column_ref.at[0, high], column_ref.at[1, high], below))
    for copies, out, forth, back in (
        (row_edges, row_edge_ref, ahead, behind),
        (column_edges, column_edge_ref, above, below),
    ):
        copies[0].wait_recv()
        relays.append(send(out.at[3, low], out.at[2, low], forth))
        copies[1].wait_recv()
        relays.append(send(out.at[1, high], out.at[2, high], back))
    for copies in (row_forward, row_backward, column_forward, column_backward):
        copies[1].wait_recv()
    for copy in relays:
        copy.wait_recv()
    for copy in spread:
        copy.wait_recv()
    for copy in started + spread + across:
        copy.wait_send()
    for copy in own_edges:
        copy.wait()
    own_total.wait()


def gather_pings(echoes, front_pick, rear_pick, rng_size):
    pings, parts, channels, length = echoes.shape
    owners = SIDE * SIDE * CORES
    block = (pings, channels, length)
    edge = (pings, channels, 128)
    bf16 = jnp.bfloat16
    copies = 3 + 8 + 4 + 8
    return pl.pallas_call(
        functools.partial(gather_kernel, rng_size),
        out_shape=(
            jax.ShapeDtypeStruct((SIDE - 1,) + block, bf16),
            jax.ShapeDtypeStruct((SIDE - 1,) + block, bf16),
            jax.ShapeDtypeStruct((SIDE,) + edge, bf16),
            jax.ShapeDtypeStruct((SIDE,) + edge, bf16),
            jax.ShapeDtypeStruct((owners, 8, 128), jnp.float32),
        ),
        in_specs=[ANY, IN_VMEM, IN_VMEM],
        out_specs=(ANY,) * 5,
        scratch_shapes=[
            pltpu.VMEM((pings + 1, parts, channels, length), bf16),
            pltpu.VMEM((2, pings, parts, channels, 128), bf16),
            pltpu.VMEM((parts,) + edge, bf16),
            pltpu.VMEM((rng_size, 8, 128), jnp.float32),
            pltpu.VMEM((8, 128), jnp.float32),
            pltpu.SemaphoreType.DMA((4,)),
            pltpu.SemaphoreType.DMA((copies,)),
            pltpu.SemaphoreType.DMA((copies,)),
            pltpu.SemaphoreType.DMA((owners + rng_size,)),
            pltpu.SemaphoreType.DMA((owners + rng_size,)),
        ],
        compiler_params=pltpu.CompilerParams(collective_id=0, has_side_effects=True),
        name="gather_pings",
    )(echoes, front_pick, rear_pick)


def window_kernel(table, echo_ref, row_ref, column_ref, row_edge_ref, column_edge_ref, out_ref, held, edge, sem):
    step = pl.program_id(0)
    pings, length = PING_DEV, held.shape[3]
    tiles = length // 128

    @pl.when(step == 0)
    def _():
        copies = []
        for part, gathered, gathered_edge in ((0, row_ref, row_edge_ref), (1, column_ref, column_edge_ref)):
            copies.append(pltpu.make_async_copy(echo_ref.at[:, part], held.at[part, 0:pings], sem.at[part, 0]))
            for d in range(1, SIDE):
                copies.append(
                    pltpu.make_async_copy(
                        gathered.at[d - 1], held.at[part, pings * d : pings * (d + 1)], sem.at[part, d]
                    )
                )
            for d in range(SIDE):
                copies.append(
                    pltpu.make_async_copy(
                        gathered_edge.at[d], edge.at[part, pings * d : pings * (d + 1)], sem.at[part, SIDE + d]
                    )
                )
        for copy in copies:
            copy.start()
        for copy in copies:
            copy.wait()

    part = step // HOLD
    lane = lax.broadcasted_iota(jnp.int32, (C, 128), 1)

    def one_slot(s, carry):
        local = table[0, step * HOLD + s]
        offset = table[1, step * HOLD + s]
        live = table[2, step * HOLD + s]

        @pl.when(live != 0)
        def _():
            back = offset < 0
            rem = jnp.where(back, offset + 128, offset)
            turn = lax.rem(128 - rem, 128)
            keep = lane < 128 - rem
            outside = edge[part, local].astype(jnp.float32)
            here = held[part, local, :, 0:128].astype(jnp.float32)
            current = pltpu.roll(jnp.where(back, outside, here), turn, 1)
            for k in range(tiles):
                ahead = (
                    held[part, local, :, 128 * (k + 1) : 128 * (k + 2)].astype(jnp.float32)
                    if k + 1 < tiles
                    else outside
                )
                following = pltpu.roll(jnp.where(back, here, ahead), turn, 1)
                out_ref[0, s, :, 128 * k : 128 * (k + 1)] = jnp.where(keep, current, following).astype(
                    jnp.bfloat16
                )
                current, here = following, ahead

        return carry

    lax.fori_loop(0, HOLD, one_slot, 0)


def cut_windows(table, echoes, row, column, row_edge, column_edge):
    pings, parts, channels, length = echoes.shape
    groups = 2 * HOLD
    return pl.pallas_call(
        window_kernel,
        out_shape=jax.ShapeDtypeStruct((groups, HOLD, channels, length), jnp.bfloat16),
        grid_spec=pltpu.PrefetchScalarGridSpec(
            num_scalar_prefetch=1,
            grid=(groups,),
            in_specs=[ANY] * 5,
            out_specs=pl.BlockSpec((1, HOLD, channels, length), lambda i, t: (i, 0, 0, 0)),
            scratch_shapes=[
                pltpu.VMEM((parts, SIDE * pings, channels, length), jnp.bfloat16),
                pltpu.VMEM((parts, SIDE * pings, channels, 128), jnp.bfloat16),
                pltpu.SemaphoreType.DMA((parts, 2 * SIDE)),
            ],
        ),
        name="cut_windows",
    )(table, echoes, row, column, row_edge, column_edge)


def turns_of(sums_ref, owner, local):
    sums = sums_ref[:, 0, :]
    owners = sums.shape[0]
    lane = lax.broadcasted_iota(jnp.int32, (owners, 128), 1)
    row = lax.broadcasted_iota(jnp.int32, (owners, 128), 0)
    front = pltpu.roll(sums, 128 - PING_DEV, 1)
    rear = pltpu.roll(sums, 128 - 2 * PING_DEV, 1)
    valid = lane < PING_DEV
    energy = jnp.where(valid, front * rear, 1.0)
    running = jnp.where(valid, sums / (jnp.sqrt(energy) + small_value), 0.0)
    step = 1
    while step < PING_DEV:
        running = running + jnp.where(lane >= step, pltpu.roll(running, step, 1), 0.0)
        step *= 2
    last = jnp.sum(jnp.where(lane == PING_DEV - 1, running, 0.0), axis=1, keepdims=True)
    before = jnp.broadcast_to(last, (owners, 128))
    step = 1
    while step < owners:
        before = before + jnp.where(row >= step, pltpu.roll(before, step, 0), 0.0)
        step *= 2
    before = jnp.where(row >= 1, pltpu.roll(before, 1, 0), 0.0)
    turn = jnp.where(valid, running + before, 0.0)
    entries = owner.shape[0]
    lane = lax.broadcasted_iota(jnp.int32, (entries, 128), 1)
    at_lane = lane == local
    picked = jnp.zeros((entries, 128), jnp.float32)
    for k in range(owners):
        picked = picked + jnp.where(at_lane & (owner == k), turn[k : k + 1, :], 0.0)
    return jnp.sum(picked, axis=1, keepdims=True)


def focus_kernel(
    table,
    slots_ref,
    sums_ref,
    list_ref,
    scale_ref,
    earlier_ref,
    out_ref,
    weights,
    stacked,
    image,
    cosines,
    sines,
    local_sem,
    send_sem,
    recv_sem,
    *received,
):
    me = lax.axis_index("ping")
    y, x, c = place(me)
    chunks, wide = len(received), stacked.shape[1]
    targets = []
    for k in range(1, HOLD):
        for part in range(2):
            d, dc = k // CORES, k % CORES
            to = device(y + d, x, c + dc) if part == 0 else device(y, x + d, c + dc)
            targets.append((part * HOLD + k, to))
    barrier = pltpu.get_barrier_semaphore()
    for _, to in targets:
        pl.semaphore_signal(barrier, inc=1, device_id={"ping": to}, device_id_type=MESH)
    own, before = [], []
    for q in range(chunks):
        for part in range(2):
            group = part * HOLD
            own.append(
                pltpu.make_async_copy(
                    slots_ref.at[group, :, :, pl.ds(q * wide, wide)],
                    received[q].at[pl.ds(group * HOLD, HOLD)],
                    local_sem.at[q, part],
                )
            )
            own[-1].start()
    for q in range(chunks):
        before.append(
            pltpu.make_async_copy(
                earlier_ref.at[:, pl.ds(q * wide, wide)], image.at[q], local_sem.at[q, 2]
            )
        )
        before[-1].start()
    pl.semaphore_wait(barrier, len(targets))
    copies = []
    for q in range(chunks):
        for i, (group, to) in enumerate(targets):
            copies.append(
                pltpu.make_async_remote_copy(
                    src_ref=slots_ref.at[group, :, :, pl.ds(q * wide, wide)],
                    dst_ref=received[q].at[pl.ds(group * HOLD, HOLD)],
                    send_sem=send_sem.at[q, i],
                    recv_sem=recv_sem.at[q, i],
                    device_id={"ping": to},
                    device_id_type=MESH,
                )
            )
            copies[-1].start()

    span = cosines.shape[1]
    along = lax.broadcasted_iota(jnp.int32, (MOST, span), 1)
    turn = turns_of(sums_ref, list_ref[:, 0:1], list_ref[:, 1:2])
    folded = list_ref[:, 2:3] + along
    folded = jnp.where(folded >= phase_modulus, folded - phase_modulus, folded)
    square = folded * folded
    square = square - phase_modulus * (
        square.astype(jnp.float32) * (1.0 / phase_modulus)
    ).astype(jnp.int32)
    square = jnp.where(square < 0, square + phase_modulus, square)
    square = jnp.where(square >= phase_modulus, square - phase_modulus, square)
    phases = square.astype(jnp.float32) * (2.0 * math.pi / phase_modulus) + (
        list_ref[:, 3:4].astype(jnp.float32) * (math.pi / 4.0) - turn
    )
    cosines[...] = jnp.cos(phases) * scale_ref[:, 0:1]
    sines[...] = jnp.sin(phases) * scale_ref[:, 0:1]

    def spread(ref, j):
        return pltpu.roll(
            jnp.broadcast_to(ref[pl.ds(j, 1), :], (C, span)),
            span - 2 * (C - 1),
            1,
            stride=2,
            stride_axis=0,
        )[:, :X]

    def weigh(pair, carry):
        upper, lower = [], []
        for s in range(2):
            cosine = spread(cosines, 2 * pair + s)
            sine = spread(sines, 2 * pair + s)
            upper += [cosine, -sine]
            lower += [sine, cosine]
        at = pl.ds(pl.multiple_of(pair * 4 * C, 4 * C), 4 * C)
        weights[0:X, at] = jnp.concatenate(upper, axis=0).T.astype(jnp.bfloat16)
        weights[X : 2 * X, at] = jnp.concatenate(lower, axis=0).T.astype(jnp.bfloat16)
        return carry

    lax.fori_loop(0, MOST // 2, weigh, 0)

    rows = X
    after = []
    for q in range(chunks):
        for copy in own[2 * q : 2 * q + 2]:
            copy.wait()
        for copy in copies[q * len(targets) : (q + 1) * len(targets)]:
            copy.wait_recv()

        def fill(j, carry):
            for part in range(2):
                at = pl.multiple_of(j * 2 * C + part * C, C)
                stacked[pl.ds(at, C), :] = received[q][table[part, j]]
            return carry

        lax.fori_loop(0, MOST, fill, 0)
        before[q].wait()

        def multiply(i, carry):
            at = pl.ds(pl.multiple_of(i * rows, rows), rows)
            product = jnp.dot(weights[at, :], stacked[...], preferred_element_type=jnp.float32)
            image[q, at, :] = (image[q, at, :].astype(jnp.float32) + product).astype(jnp.bfloat16)
            return carry

        lax.fori_loop(0, 2 * X // rows, multiply, 0)
        after.append(
            pltpu.make_async_copy(
                image.at[q], out_ref.at[:, pl.ds(q * wide, wide)], local_sem.at[q, 3]
            )
        )
        after[-1].start()
    for copy in copies:
        copy.wait_send()
    for copy in after:
        copy.wait()


def focus(table, slots, sums, entries, scales, earlier):
    groups, hold, channels, length = slots.shape
    chunks = 4
    wide = length // chunks
    count = groups - 2
    return pl.pallas_call(
        focus_kernel,
        out_shape=jax.ShapeDtypeStruct((2 * X, length), jnp.bfloat16),
        in_specs=[pl.BlockSpec(memory_space=pltpu.SMEM), ANY, IN_VMEM, IN_VMEM, IN_VMEM, ANY],
        out_specs=ANY,
        scratch_shapes=[
            pltpu.VMEM((2 * X, MOST * 2 * C), jnp.bfloat16),
            pltpu.VMEM((MOST * 2 * C, wide), jnp.bfloat16),
            pltpu.VMEM((chunks, 2 * X, wide), jnp.bfloat16),
            pltpu.VMEM((MOST, X + 128), jnp.float32),
            pltpu.VMEM((MOST, X + 128), jnp.float32),
            pltpu.SemaphoreType.DMA((chunks, 4)),
            pltpu.SemaphoreType.DMA((chunks, count)),
            pltpu.SemaphoreType.DMA((chunks, count)),
        ]
        + [pltpu.VMEM((groups * hold, channels, wide), jnp.bfloat16)] * chunks,
        compiler_params=pltpu.CompilerParams(
            collective_id=1, has_side_effects=True, vmem_limit_bytes=60 << 20
        ),
        name="focus",
    )(table, slots, sums, entries, scales, earlier)


def rank_in(groups, positions):
    same = (groups[:, None, :] == groups[:, :, None]) & (positions[None, :] < positions[:, None])[None]
    return jnp.sum(same.astype(jnp.int32), axis=2)


def per_device(echoes, pairing, footprint, counts, offsets, earlier):
    block_len = echoes.shape[3]
    owners = lax.axis_size("ping")
    rng_size = lax.axis_size("rng")
    me = lax.axis_index("ping")
    y, x, c = place(me)

    channel_ids = jnp.arange(C, dtype=jnp.int32)
    front_pick = (pairing[:, 0, :, None] == channel_ids).astype(jnp.bfloat16)
    rear_pick = (pairing[:, 1, :, None] == channel_ids).astype(jnp.bfloat16)
    row, column, row_edge, column_edge, sums = gather_pings(echoes, front_pick, rear_pick, rng_size)

    steps = jnp.arange(HOLD, dtype=jnp.int32)
    tiles = jnp.concatenate(
        [
            device(y + steps // CORES, x, c + steps % CORES),
            device(y, x + steps // CORES, c + steps % CORES),
        ]
    )
    all_tiles = jnp.arange(owners, dtype=jnp.int32)
    chosen = (tiles[:, None] == all_tiles[None, :]).astype(jnp.int32)
    positions = jnp.arange(MOST, dtype=jnp.int32)
    foot = jnp.sum(chosen[:, :, None] * footprint[None], axis=1)
    shift = jnp.sum(chosen[:, :, None] * offsets[None], axis=1)
    count = jnp.sum(chosen * counts[None, :], axis=1)
    listed = positions[None, :] < count[:, None]
    oy, ox, oc = place(foot // PING_DEV)
    by_row = steps[:, None] >= 0
    by_row = jnp.concatenate([by_row, ~by_row], axis=0)
    group = jnp.where(listed, jnp.where(by_row, oy, ox) * CORES + oc, -1)
    rank = rank_in(group, positions)
    here = group == jnp.where(by_row, y, x) * CORES + c
    distance = jnp.where(by_row, ox - x + SIDE, oy - y + SIDE) % SIDE
    source = distance * PING_DEV + foot % PING_DEV
    fits = (here[:, None, :] & (rank[:, None, :] == steps[None, :, None])).astype(jnp.int32)
    table = jnp.stack(
        [
            jnp.sum(fits * source[:, None, :], axis=2).reshape(-1),
            jnp.sum(fits * shift[:, None, :], axis=2).reshape(-1),
            jnp.sum(fits, axis=2).reshape(-1),
        ]
    )
    slots = cut_windows(table, echoes, row, column, row_edge, column_edge)

    own_group = jnp.stack([group[0], group[HOLD]])
    own_rank = jnp.stack([rank[0], rank[HOLD]])
    own_place = jnp.stack([y, x])[:, None]
    own_distance = (own_place - own_group // CORES + SIDE) % SIDE
    own_core = (c - own_group % CORES + CORES) % CORES
    arrival = (own_distance * CORES + own_core) * HOLD + own_rank
    arrival = jnp.where(listed[0:1], arrival, arrival[:, 0:1])
    arrival = arrival + jnp.array([[0], [HOLD * HOLD]], jnp.int32)
    entries = jnp.stack(
        [
            foot[0] // PING_DEV,
            foot[0] % PING_DEV,
            jnp.remainder(me * X - foot[0] * SPACING - 2 * (C - 1), phase_modulus),
            shift[0],
        ],
        axis=1,
    )
    scales = listed[0].astype(jnp.float32) / jnp.sqrt(jnp.float32(C) * count[0].astype(jnp.float32))
    image = focus(arrival, slots, sums, entries, scales[:, None], earlier.reshape(2 * X, block_len))
    return image.reshape(earlier.shape)


def solution(mesh):
    return jax.shard_map(
        per_device,
        mesh=mesh,
        in_specs=(
            P("ping", None, None, "rng"),
            P("ping", None, None),
            P(),
            P(),
            P(),
            P("ping", None, None, "rng"),
        ),
        out_specs=P("ping", None, None, "rng"),
        check_vma=False,
    )
```

```python
import functools
import math

import jax
import jax.numpy as jnp
from jax import lax
from jax.experimental import pallas as pl
from jax.experimental.pallas import tpu as pltpu
from jax.sharding import PartitionSpec as P

C = 32
X = 1024
MOST = 48
PING_DEV = 16
SPACING = X // PING_DEV
SIDE = 4
CORES = 2
HOLD = 8
MESH = pl.DeviceIdType.MESH
ANY = pl.BlockSpec(memory_space=pl.ANY)
IN_VMEM = pl.BlockSpec(memory_space=pltpu.VMEM)

phase_modulus = 4099
small_value = 1e-06


def place(index):
    return index // (SIDE * CORES), (index // CORES) % SIDE, index % CORES


def device(y, x, c):
    return (((y + SIDE) % SIDE) * SIDE + (x + SIDE) % SIDE) * CORES + (c + CORES) % CORES


def turns_of(sums_ref, owner, local):
    sums = sums_ref[:, 0, :]
    owners = sums.shape[0]
    lane = lax.broadcasted_iota(jnp.int32, (owners, 128), 1)
    row = lax.broadcasted_iota(jnp.int32, (owners, 128), 0)
    front = pltpu.roll(sums, 128 - PING_DEV, 1)
    rear = pltpu.roll(sums, 128 - 2 * PING_DEV, 1)
    valid = lane < PING_DEV
    energy = jnp.where(valid, front * rear, 1.0)
    running = jnp.where(valid, sums / (jnp.sqrt(energy) + small_value), 0.0)
    step = 1
    while step < PING_DEV:
        running = running + jnp.where(lane >= step, pltpu.roll(running, step, 1), 0.0)
        step *= 2
    last = jnp.sum(jnp.where(lane == PING_DEV - 1, running, 0.0), axis=1, keepdims=True)
    before = jnp.broadcast_to(last, (owners, 128))
    step = 1
    while step < owners:
        before = before + jnp.where(row >= step, pltpu.roll(before, step, 0), 0.0)
        step *= 2
    before = jnp.where(row >= 1, pltpu.roll(before, 1, 0), 0.0)
    turn = jnp.where(valid, running + before, 0.0)
    entries = owner.shape[0]
    lane = lax.broadcasted_iota(jnp.int32, (entries, 128), 1)
    at_lane = lane == local
    picked = jnp.zeros((entries, 128), jnp.float32)
    for k in range(owners):
        picked = picked + jnp.where(at_lane & (owner == k), turn[k : k + 1, :], 0.0)
    return jnp.sum(picked, axis=1, keepdims=True)


def image_kernel(
    rng_size,
    table,
    arrival,
    echo_ref,
    front_ref,
    rear_ref,
    list_ref,
    scale_ref,
    earlier_ref,
    out_ref,
    row_pings,
    column_pings,
    row_edges,
    column_edges,
    lead,
    beside,
    partial,
    total,
    sums,
    staging,
    weights,
    stacked,
    image,
    cosines,
    sines,
    local_sem,
    send_sem,
    recv_sem,
    sum_send,
    sum_recv,
    slot_send,
    slot_recv,
    *received,
):
    me = lax.axis_index("ping")
    level = lax.axis_index("rng")
    y, x, c = place(me)
    owners = SIDE * SIDE * CORES
    pings, half = PING_DEV, PING_DEV // 2
    length = echo_ref.shape[3]
    chunks, wide = len(received), stacked.shape[1]

    barrier = pltpu.get_barrier_semaphore()
    for step in range(1, owners):
        pl.semaphore_signal(
            barrier, inc=1, device_id={"ping": (me + step) % owners}, device_id_type=MESH
        )
    for step in range(1, rng_size):
        pl.semaphore_signal(
            barrier, inc=1, device_id={"rng": (level + step) % rng_size}, device_id_type=MESH
        )
    own = [
        pltpu.make_async_copy(echo_ref.at[:, 0], row_pings.at[pl.ds(0, pings)], local_sem.at[0]),
        pltpu.make_async_copy(echo_ref.at[:, 1], column_pings.at[pl.ds(0, pings)], local_sem.at[1]),
    ]
    before = [
        pltpu.make_async_copy(
            earlier_ref.at[:, pl.ds(q * wide, wide)], image.at[q % 2], local_sem.at[2 + q]
        )
        for q in range(chunks)
    ]
    after = [
        pltpu.make_async_copy(
            image.at[q % 2], out_ref.at[:, pl.ds(q * wide, wide)], local_sem.at[2 + chunks + q]
        )
        for q in range(chunks)
    ]
    for copy in own + before[:2]:
        copy.start()
    pl.semaphore_wait(barrier, owners + rng_size - 2)

    started = []

    def send(src, dst, target):
        i = len(started)
        copy = pltpu.make_async_remote_copy(
            src_ref=src,
            dst_ref=dst,
            send_sem=send_sem.at[i],
            recv_sem=recv_sem.at[i],
            device_id=target,
            device_id_type=MESH,
        )
        copy.start()
        started.append(copy)
        return copy

    up, down = {"rng": (level + 1) % rng_size}, {"rng": (level + rng_size - 1) % rng_size}
    ahead = {"ping": device(y, x + 1, c)}
    behind = {"ping": device(y, x - 1, c)}
    above = {"ping": device(y + 1, x, c)}
    below = {"ping": device(y - 1, x, c)}
    low, high = pl.ds(0, half), pl.ds(half, half)

    def part_of(distance, start):
        return pl.ds(distance * pings + start, half)

    from_lead = send(echo_ref.at[pings - 1], lead, {"ping": (me + 1) % owners})
    from_low = send(echo_ref.at[:, :, :, pl.ds(length - 128, 128)], beside.at[0], up)
    from_high = send(echo_ref.at[:, :, :, pl.ds(0, 128)], beside.at[1], down)
    forward, backward = [], []
    for turn in range(2):
        for part, pool, forth, back in (
            (0, row_pings, ahead, behind),
            (1, column_pings, above, below),
        ):
            first, second = (low, high) if turn == 0 else (high, low)
            forward.append(
                send(echo_ref.at[first, part], pool.at[part_of(3, turn * half)], forth)
            )
            backward.append(
                send(echo_ref.at[second, part], pool.at[part_of(1, (1 - turn) * half)], back)
            )

    from_low.wait_recv()
    from_high.wait_recv()
    lane = lax.broadcasted_iota(jnp.int32, (C, 128), 1)
    use_low = level > 0
    use_high = level < rng_size - 1
    pools = (row_pings, column_pings)
    rims = (row_edges, column_edges)

    def merge(p, carry):
        for part in range(2):
            low_edge = beside[0, p, part].astype(jnp.float32)
            high_edge = beside[1, p, part].astype(jnp.float32)
            merged = jnp.where(
                lane < 64,
                jnp.where(use_high, high_edge, 0.0),
                jnp.where(use_low, low_edge, 0.0),
            )
            rims[part][p] = merged.astype(jnp.bfloat16)
        return carry

    lax.fori_loop(0, pings, merge, 0)

    for copy in own:
        copy.wait()
    from_lead.wait_recv()
    place_lane = lax.broadcasted_iota(jnp.int32, (8, 128), 1)

    def fold(value):
        out = value[:, 0:128]
        for k in range(1, length // 128):
            out = out + value[:, 128 * k : 128 * (k + 1)]
        out = jnp.sum(out, axis=0, keepdims=True)
        return jnp.sum(out, axis=1, keepdims=True)

    def correlate(p, front_source, acc):
        front, rear = front_ref[p], rear_ref[p]
        dot = functools.partial(jnp.dot, preferred_element_type=jnp.float32)
        front_real = dot(front, front_source[0])
        front_imag = dot(front, front_source[1])
        rear_real = dot(rear, row_pings[p])
        rear_imag = dot(rear, column_pings[p])
        acc = jnp.where(place_lane == p, fold(front_real * rear_imag - front_imag * rear_real), acc)
        acc = jnp.where(
            place_lane == p + pings, fold(front_real * front_real + front_imag * front_imag), acc
        )
        return jnp.where(
            place_lane == p + 2 * pings, fold(rear_real * rear_real + rear_imag * rear_imag), acc
        )

    mine = correlate(0, (lead[0], lead[1]), jnp.zeros((8, 128), jnp.float32))
    mine = jnp.where((me == 0) & (place_lane < 2 * pings), 0.0, mine)
    mine = lax.fori_loop(
        1, pings, lambda p, acc: correlate(p, (row_pings[p - 1], column_pings[p - 1]), acc), mine
    )
    partial[0] = mine

    edge_forward = [
        send(rims[part].at[pl.ds(0, pings)], rims[part].at[pl.ds(3 * pings, pings)], forth)
        for part, forth in ((0, ahead), (1, above))
    ]
    edge_backward = [
        send(rims[part].at[pl.ds(0, pings)], rims[part].at[pl.ds(pings, pings)], back)
        for part, back in ((0, behind), (1, below))
    ]
    across = []
    for step in range(1, rng_size):
        across.append(
            pltpu.make_async_remote_copy(
                src_ref=partial.at[0],
                dst_ref=partial.at[step],
                send_sem=sum_send.at[owners + step],
                recv_sem=sum_recv.at[owners + step],
                device_id={"rng": (level + step) % rng_size},
                device_id_type=MESH,
            )
        )
        across[-1].start()
    for copy in across:
        copy.wait_recv()
    whole = mine
    for step in range(1, rng_size):
        whole = whole + partial[step]
    total[...] = whole
    sums[me] = whole
    spread_sums = []
    for step in range(1, owners):
        spread_sums.append(
            pltpu.make_async_remote_copy(
                src_ref=total,
                dst_ref=sums.at[me],
                send_sem=sum_send.at[step],
                recv_sem=sum_recv.at[step],
                device_id={"ping": (me + step) % owners},
                device_id_type=MESH,
            )
        )
        spread_sums[-1].start()

    relays = []
    for part, forth, back in ((0, ahead, behind), (1, above, below)):
        pool, rim = pools[part], rims[part]
        forward[part].wait_recv()
        relays.append(send(pool.at[part_of(3, 0)], pool.at[part_of(2, 0)], forth))
        backward[part].wait_recv()
        relays.append(send(pool.at[part_of(1, half)], pool.at[part_of(2, half)], back))
    for part, forth, back in ((0, ahead, behind), (1, above, below)):
        pool, rim = pools[part], rims[part]
        edge_forward[part].wait_recv()
        relays.append(send(rim.at[part_of(3, 0)], rim.at[part_of(2, 0)], forth))
        edge_backward[part].wait_recv()
        relays.append(send(rim.at[part_of(1, half)], rim.at[part_of(2, half)], back))
    for copy in spread_sums:
        copy.wait_recv()

    span = cosines.shape[1]
    along = lax.broadcasted_iota(jnp.int32, (MOST, span), 1)
    turn = turns_of(sums, list_ref[:, 0:1], list_ref[:, 1:2])
    folded = list_ref[:, 2:3] + along
    folded = jnp.where(folded >= phase_modulus, folded - phase_modulus, folded)
    square = folded * folded
    square = square - phase_modulus * (
        square.astype(jnp.float32) * (1.0 / phase_modulus)
    ).astype(jnp.int32)
    square = jnp.where(square < 0, square + phase_modulus, square)
    square = jnp.where(square >= phase_modulus, square - phase_modulus, square)
    phases = square.astype(jnp.float32) * (2.0 * math.pi / phase_modulus) + (
        list_ref[:, 3:4].astype(jnp.float32) * (math.pi / 4.0) - turn
    )
    cosines[...] = jnp.cos(phases) * scale_ref[:, 0:1]
    sines[...] = jnp.sin(phases) * scale_ref[:, 0:1]

    def spread(ref, j):
        return pltpu.roll(
            jnp.broadcast_to(ref[pl.ds(j, 1), :], (C, span)),
            span - 2 * (C - 1),
            1,
            stride=2,
            stride_axis=0,
        )[:, :X]

    def weigh(pair, carry):
        upper, lower = [], []
        for s in range(2):
            cosine = spread(cosines, 2 * pair + s)
            sine = spread(sines, 2 * pair + s)
            upper += [cosine, -sine]
            lower += [sine, cosine]
        at = pl.ds(pl.multiple_of(pair * 4 * C, 4 * C), 4 * C)
        weights[0:X, at] = jnp.concatenate(upper, axis=0).T.astype(jnp.bfloat16)
        weights[X : 2 * X, at] = jnp.concatenate(lower, axis=0).T.astype(jnp.bfloat16)
        return carry

    lax.fori_loop(0, MOST // 2, weigh, 0)

    for copy in forward[2:] + backward[2:] + relays:
        copy.wait_recv()

    targets = []
    for k in range(1, HOLD):
        for part in range(2):
            d, dc = k // CORES, k % CORES
            to = device(y + d, x, c + dc) if part == 0 else device(y, x + d, c + dc)
            targets.append((part * HOLD + k, to))
    tiles = length // 128

    def cut(q, part, slot):
        local = table[0, part * HOLD * HOLD + slot]
        offset = table[1, part * HOLD * HOLD + slot]
        pool = pools[part]
        back = offset < 0
        rem = jnp.where(back, offset + 128, offset)
        turn = lax.rem(128 - rem, 128)
        keep = lane < 128 - rem
        first = q * wide // 128

        def tile(k):
            if k < 0 or k >= tiles:
                return rims[part][local].astype(jnp.float32)
            return pool[local, :, 128 * k : 128 * (k + 1)].astype(jnp.float32)

        here = tile(first)
        current = pltpu.roll(jnp.where(back, tile(first - 1), here), turn, 1)
        out = []
        for k in range(first, first + wide // 128):
            following_tile = tile(k + 1)
            following = pltpu.roll(jnp.where(back, here, following_tile), turn, 1)
            out.append(jnp.where(keep, current, following).astype(jnp.bfloat16))
            current, here = following, following_tile
        return out

    def build(q):
        for part in range(2):

            def for_self(s, carry):
                for k, value in enumerate(cut(q, part, s)):
                    received[q][part * HOLD * HOLD + s, :, 128 * k : 128 * (k + 1)] = value
                return carry

            def for_others(s, carry):
                for k, value in enumerate(cut(q, part, s)):
                    staging[q % 2, part * HOLD * HOLD + s, :, 128 * k : 128 * (k + 1)] = value
                return carry

            lax.fori_loop(0, HOLD, for_self, 0)
            lax.fori_loop(HOLD, HOLD * HOLD, for_others, 0)

    def ship(q):
        copies = []
        for i, (group, to) in enumerate(targets):
            at = pl.ds(group * HOLD, HOLD)
            copies.append(
                pltpu.make_async_remote_copy(
                    src_ref=staging.at[q % 2, at],
                    dst_ref=received[q].at[at],
                    send_sem=slot_send.at[q, i],
                    recv_sem=slot_recv.at[q, i],
                    device_id={"ping": to},
                    device_id_type=MESH,
                )
            )
            copies[-1].start()
        return copies

    shipped = []
    for q in range(2):
        build(q)
        shipped.append(ship(q))
    rows = X
    for q in range(chunks):
        if q + 2 < chunks:
            for copy in shipped[q]:
                copy.wait_send()
            build(q + 2)
            shipped.append(ship(q + 2))
        for copy in shipped[q]:
            copy.wait_recv()

        def fill(j, carry):
            for part in range(2):
                at = pl.multiple_of(j * 2 * C + part * C, C)
                stacked[pl.ds(at, C), :] = received[q][arrival[part, j]]
            return carry

        lax.fori_loop(0, MOST, fill, 0)
        before[q].wait()

        def multiply(i, carry):
            at = pl.ds(pl.multiple_of(i * rows, rows), rows)
            product = jnp.dot(weights[at, :], stacked[...], preferred_element_type=jnp.float32)
            image[q % 2, at, :] = (image[q % 2, at, :].astype(jnp.float32) + product).astype(
                jnp.bfloat16
            )
            return carry

        lax.fori_loop(0, 2 * X // rows, multiply, 0)
        after[q].start()
        if q >= 1 and q + 1 < chunks:
            after[q - 1].wait()
            before[q + 1].start()
    for copy in started + across + spread_sums + shipped[chunks - 2] + shipped[chunks - 1]:
        copy.wait_send()
    for copy in after[chunks - 2 :]:
        copy.wait()


def focus(table, arrival, echoes, front_pick, rear_pick, entries, scales, earlier, rng_size):
    pings, parts, channels, length = echoes.shape
    owners = SIDE * SIDE * CORES
    chunks = 8
    wide = length // chunks
    slots = 2 * HOLD * HOLD
    count = 2 * (HOLD - 1)
    bf16, f32 = jnp.bfloat16, jnp.float32
    dma = pltpu.SemaphoreType.DMA
    steps = 3 + 8 + 4 + 8
    smem = pl.BlockSpec(memory_space=pltpu.SMEM)
    return pl.pallas_call(
        functools.partial(image_kernel, rng_size),
        out_shape=jax.ShapeDtypeStruct((2 * X, length), bf16),
        in_specs=[smem, smem, ANY, IN_VMEM, IN_VMEM, IN_VMEM, IN_VMEM, ANY],
        out_specs=ANY,
        scratch_shapes=[
            pltpu.VMEM((SIDE * pings, channels, length), bf16),
            pltpu.VMEM((SIDE * pings, channels, length), bf16),
            pltpu.VMEM((SIDE * pings, channels, 128), bf16),
            pltpu.VMEM((SIDE * pings, channels, 128), bf16),
            pltpu.VMEM((parts, channels, length), bf16),
            pltpu.VMEM((2, pings, parts, channels, 128), bf16),
            pltpu.VMEM((rng_size, 8, 128), f32),
            pltpu.VMEM((8, 128), f32),
            pltpu.VMEM((owners, 8, 128), f32),
            pltpu.VMEM((2, slots, channels, wide), bf16),
            pltpu.VMEM((2 * X, MOST * 2 * C), bf16),
            pltpu.VMEM((MOST * 2 * C, wide), bf16),
            pltpu.VMEM((2, 2 * X, wide), bf16),
            pltpu.VMEM((MOST, X + 128), f32),
            pltpu.VMEM((MOST, X + 128), f32),
            dma((2 + 2 * chunks,)),
            dma((steps,)),
            dma((steps,)),
            dma((owners + rng_size,)),
            dma((owners + rng_size,)),
            dma((chunks, count)),
            dma((chunks, count)),
        ]
        + [pltpu.VMEM((slots, channels, wide), bf16)] * chunks,
        compiler_params=pltpu.CompilerParams(
            collective_id=0, has_side_effects=True, vmem_limit_bytes=63 << 20
        ),
        name="focus",
    )(table, arrival, echoes, front_pick, rear_pick, entries, scales, earlier)


def rank_in(groups, positions):
    same = (groups[:, None, :] == groups[:, :, None]) & (positions[None, :] < positions[:, None])[None]
    return jnp.sum(same.astype(jnp.int32), axis=2)


def per_device(echoes, pairing, footprint, counts, offsets, earlier):
    block_len = echoes.shape[3]
    owners = lax.axis_size("ping")
    rng_size = lax.axis_size("rng")
    me = lax.axis_index("ping")
    y, x, c = place(me)

    channel_ids = jnp.arange(C, dtype=jnp.int32)
    front_pick = (pairing[:, 0, :, None] == channel_ids).astype(jnp.bfloat16)
    rear_pick = (pairing[:, 1, :, None] == channel_ids).astype(jnp.bfloat16)

    steps = jnp.arange(HOLD, dtype=jnp.int32)
    tiles = jnp.concatenate(
        [
            device(y + steps // CORES, x, c + steps % CORES),
            device(y, x + steps // CORES, c + steps % CORES),
        ]
    )
    all_tiles = jnp.arange(owners, dtype=jnp.int32)
    chosen = (tiles[:, None] == all_tiles[None, :]).astype(jnp.int32)
    positions = jnp.arange(MOST, dtype=jnp.int32)
    foot = jnp.sum(chosen[:, :, None] * footprint[None], axis=1)
    shift = jnp.sum(chosen[:, :, None] * offsets[None], axis=1)
    count = jnp.sum(chosen * counts[None, :], axis=1)
    listed = positions[None, :] < count[:, None]
    oy, ox, oc = place(foot // PING_DEV)
    by_row = steps[:, None] >= 0
    by_row = jnp.concatenate([by_row, ~by_row], axis=0)
    group = jnp.where(listed, jnp.where(by_row, oy, ox) * CORES + oc, -1)
    rank = rank_in(group, positions)
    here = group == jnp.where(by_row, y, x) * CORES + c
    distance = jnp.where(by_row, ox - x + SIDE, oy - y + SIDE) % SIDE
    source = distance * PING_DEV + foot % PING_DEV
    fits = (here[:, None, :] & (rank[:, None, :] == steps[None, :, None])).astype(jnp.int32)
    table = jnp.stack(
        [
            jnp.sum(fits * source[:, None, :], axis=2).reshape(-1),
            jnp.sum(fits * shift[:, None, :], axis=2).reshape(-1),
        ]
    )
    own_group = jnp.stack([group[0], group[HOLD]])
    own_rank = jnp.stack([rank[0], rank[HOLD]])
    own_place = jnp.stack([y, x])[:, None]
    own_distance = (own_place - own_group // CORES + SIDE) % SIDE
    own_core = (c - own_group % CORES + CORES) % CORES
    arrival = (own_distance * CORES + own_core) * HOLD + own_rank
    arrival = jnp.where(listed[0:1], arrival, arrival[:, 0:1])
    arrival = arrival + jnp.array([[0], [HOLD * HOLD]], jnp.int32)
    entries = jnp.stack(
        [
            foot[0] // PING_DEV,
            foot[0] % PING_DEV,
            jnp.remainder(me * X - foot[0] * SPACING - 2 * (C - 1), phase_modulus),
            shift[0],
        ],
        axis=1,
    )
    scales = listed[0].astype(jnp.float32) / jnp.sqrt(jnp.float32(C) * count[0].astype(jnp.float32))
    image = focus(
        table,
        arrival,
        echoes,
        front_pick,
        rear_pick,
        entries,
        scales[:, None],
        earlier.reshape(2 * X, block_len),
        rng_size,
    )
    return image.reshape(earlier.shape)


def solution(mesh):
    return jax.shard_map(
        per_device,
        mesh=mesh,
        in_specs=(
            P("ping", None, None, "rng"),
            P("ping", None, None),
            P(),
            P(),
            P(),
            P("ping", None, None, "rng"),
        ),
        out_specs=P("ping", None, None, "rng"),
        check_vma=False,
    )
```

```python
import functools
import math

import jax
import jax.numpy as jnp
from jax import lax
from jax.experimental import pallas as pl
from jax.experimental.pallas import tpu as pltpu
from jax.sharding import PartitionSpec as P

C = 32
X = 1024
MOST = 48
PING_DEV = 16
SPACING = X // PING_DEV
SIDE = 4
CORES = 2
HOLD = 8
MESH = pl.DeviceIdType.MESH
ANY = pl.BlockSpec(memory_space=pl.ANY)
IN_VMEM = pl.BlockSpec(memory_space=pltpu.VMEM)

phase_modulus = 4099
small_value = 1e-06


def place(index):
    return index // (SIDE * CORES), (index // CORES) % SIDE, index % CORES


def device(y, x, c):
    return (((y + SIDE) % SIDE) * SIDE + (x + SIDE) % SIDE) * CORES + (c + CORES) % CORES


def turns_of(sums_ref, owner, local):
    sums = sums_ref[:, 0, :]
    owners = sums.shape[0]
    lane = lax.broadcasted_iota(jnp.int32, (owners, 128), 1)
    row = lax.broadcasted_iota(jnp.int32, (owners, 128), 0)
    front = pltpu.roll(sums, 128 - PING_DEV, 1)
    rear = pltpu.roll(sums, 128 - 2 * PING_DEV, 1)
    valid = lane < PING_DEV
    energy = jnp.where(valid, front * rear, 1.0)
    running = jnp.where(valid, sums / (jnp.sqrt(energy) + small_value), 0.0)
    step = 1
    while step < PING_DEV:
        running = running + jnp.where(lane >= step, pltpu.roll(running, step, 1), 0.0)
        step *= 2
    last = jnp.sum(jnp.where(lane == PING_DEV - 1, running, 0.0), axis=1, keepdims=True)
    before = jnp.broadcast_to(last, (owners, 128))
    step = 1
    while step < owners:
        before = before + jnp.where(row >= step, pltpu.roll(before, step, 0), 0.0)
        step *= 2
    before = jnp.where(row >= 1, pltpu.roll(before, 1, 0), 0.0)
    turn = jnp.where(valid, running + before, 0.0)
    entries = owner.shape[0]
    lane = lax.broadcasted_iota(jnp.int32, (entries, 128), 1)
    at_lane = lane == local
    picked = jnp.zeros((entries, 128), jnp.float32)
    for k in range(owners):
        picked = picked + jnp.where(at_lane & (owner == k), turn[k : k + 1, :], 0.0)
    return jnp.sum(picked, axis=1, keepdims=True)


def image_kernel(
    rng_size,
    table,
    arrival,
    echo_ref,
    front_ref,
    rear_ref,
    list_ref,
    scale_ref,
    earlier_ref,
    out_ref,
    row_pings,
    column_pings,
    row_edges,
    column_edges,
    lead,
    beside,
    partial,
    total,
    sums,
    staging,
    weights,
    stacked,
    image,
    cosines,
    sines,
    local_sem,
    send_sem,
    recv_sem,
    sum_send,
    sum_recv,
    slot_send,
    slot_recv,
    *received,
):
    me = lax.axis_index("ping")
    level = lax.axis_index("rng")
    y, x, c = place(me)
    owners = SIDE * SIDE * CORES
    pings, half = PING_DEV, PING_DEV // 2
    length = echo_ref.shape[3]
    chunks, wide = len(received), stacked.shape[1]

    barrier = pltpu.get_barrier_semaphore()
    for step in range(1, owners):
        pl.semaphore_signal(
            barrier, inc=1, device_id={"ping": (me + step) % owners}, device_id_type=MESH
        )
    for step in range(1, rng_size):
        pl.semaphore_signal(
            barrier, inc=1, device_id={"rng": (level + step) % rng_size}, device_id_type=MESH
        )
    own = [
        pltpu.make_async_copy(echo_ref.at[:, 0], row_pings.at[pl.ds(0, pings)], local_sem.at[0]),
        pltpu.make_async_copy(echo_ref.at[:, 1], column_pings.at[pl.ds(0, pings)], local_sem.at[1]),
    ]
    before = [
        pltpu.make_async_copy(
            earlier_ref.at[:, pl.ds(q * wide, wide)], image.at[q % 2], local_sem.at[2 + q]
        )
        for q in range(chunks)
    ]
    after = [
        pltpu.make_async_copy(
            image.at[q % 2], out_ref.at[:, pl.ds(q * wide, wide)], local_sem.at[2 + chunks + q]
        )
        for q in range(chunks)
    ]
    for copy in own + before[:2]:
        copy.start()
    pl.semaphore_wait(barrier, owners + rng_size - 2)

    started = []

    def send(src, dst, target):
        i = len(started)
        copy = pltpu.make_async_remote_copy(
            src_ref=src,
            dst_ref=dst,
            send_sem=send_sem.at[i],
            recv_sem=recv_sem.at[i],
            device_id=target,
            device_id_type=MESH,
        )
        copy.start()
        started.append(copy)
        return copy

    up, down = {"rng": (level + 1) % rng_size}, {"rng": (level + rng_size - 1) % rng_size}
    ahead = {"ping": device(y, x + 1, c)}
    behind = {"ping": device(y, x - 1, c)}
    above = {"ping": device(y + 1, x, c)}
    below = {"ping": device(y - 1, x, c)}
    low, high = pl.ds(0, half), pl.ds(half, half)

    def part_of(distance, start):
        return pl.ds(distance * pings + start, half)

    from_lead = send(echo_ref.at[pings - 1], lead, {"ping": (me + 1) % owners})
    from_low = send(echo_ref.at[:, :, :, pl.ds(length - 128, 128)], beside.at[0], up)
    from_high = send(echo_ref.at[:, :, :, pl.ds(0, 128)], beside.at[1], down)
    forward, backward = [], []
    for turn in range(2):
        for part, pool, forth, back in (
            (0, row_pings, ahead, behind),
            (1, column_pings, above, below),
        ):
            first, second = (low, high) if turn == 0 else (high, low)
            forward.append(
                send(echo_ref.at[first, part], pool.at[part_of(3, turn * half)], forth)
            )
            backward.append(
                send(echo_ref.at[second, part], pool.at[part_of(1, (1 - turn) * half)], back)
            )

    from_low.wait_recv()
    from_high.wait_recv()
    lane = lax.broadcasted_iota(jnp.int32, (C, 128), 1)
    use_low = level > 0
    use_high = level < rng_size - 1
    pools = (row_pings, column_pings)
    rims = (row_edges, column_edges)

    def merge(p, carry):
        for part in range(2):
            low_edge = beside[0, p, part].astype(jnp.float32)
            high_edge = beside[1, p, part].astype(jnp.float32)
            merged = jnp.where(
                lane < 64,
                jnp.where(use_high, high_edge, 0.0),
                jnp.where(use_low, low_edge, 0.0),
            )
            rims[part][p] = merged.astype(jnp.bfloat16)
        return carry

    lax.fori_loop(0, pings, merge, 0)

    for copy in own:
        copy.wait()
    from_lead.wait_recv()
    place_lane = lax.broadcasted_iota(jnp.int32, (8, 128), 1)

    def fold(value):
        out = value[:, 0:128]
        for k in range(1, length // 128):
            out = out + value[:, 128 * k : 128 * (k + 1)]
        out = jnp.sum(out, axis=0, keepdims=True)
        return jnp.sum(out, axis=1, keepdims=True)

    def correlate(p, front_source, acc):
        front, rear = front_ref[p], rear_ref[p]
        dot = functools.partial(jnp.dot, preferred_element_type=jnp.float32)
        front_real = dot(front, front_source[0])
        front_imag = dot(front, front_source[1])
        rear_real = dot(rear, row_pings[p])
        rear_imag = dot(rear, column_pings[p])
        acc = jnp.where(place_lane == p, fold(front_real * rear_imag - front_imag * rear_real), acc)
        acc = jnp.where(
            place_lane == p + pings, fold(front_real * front_real + front_imag * front_imag), acc
        )
        return jnp.where(
            place_lane == p + 2 * pings, fold(rear_real * rear_real + rear_imag * rear_imag), acc
        )

    mine = correlate(0, (lead[0], lead[1]), jnp.zeros((8, 128), jnp.float32))
    mine = jnp.where((me == 0) & (place_lane < 2 * pings), 0.0, mine)
    mine = lax.fori_loop(
        1, pings, lambda p, acc: correlate(p, (row_pings[p - 1], column_pings[p - 1]), acc), mine
    )
    partial[0] = mine

    edge_forward = [
        send(rims[part].at[pl.ds(0, pings)], rims[part].at[pl.ds(3 * pings, pings)], forth)
        for part, forth in ((0, ahead), (1, above))
    ]
    edge_backward = [
        send(rims[part].at[pl.ds(0, pings)], rims[part].at[pl.ds(pings, pings)], back)
        for part, back in ((0, behind), (1, below))
    ]
    across = []
    for step in range(1, rng_size):
        across.append(
            pltpu.make_async_remote_copy(
                src_ref=partial.at[0],
                dst_ref=partial.at[step],
                send_sem=sum_send.at[owners + step],
                recv_sem=sum_recv.at[owners + step],
                device_id={"rng": (level + step) % rng_size},
                device_id_type=MESH,
            )
        )
        across[-1].start()
    for copy in across:
        copy.wait_recv()
    whole = mine
    for step in range(1, rng_size):
        whole = whole + partial[step]
    total[...] = whole
    sums[me] = whole
    spread_sums = []
    for step in range(1, owners):
        spread_sums.append(
            pltpu.make_async_remote_copy(
                src_ref=total,
                dst_ref=sums.at[me],
                send_sem=sum_send.at[step],
                recv_sem=sum_recv.at[step],
                device_id={"ping": (me + step) % owners},
                device_id_type=MESH,
            )
        )
        spread_sums[-1].start()

    relays = []
    for part, forth, back in ((0, ahead, behind), (1, above, below)):
        pool, rim = pools[part], rims[part]
        forward[part].wait_recv()
        relays.append(send(pool.at[part_of(3, 0)], pool.at[part_of(2, 0)], forth))
        backward[part].wait_recv()
        relays.append(send(pool.at[part_of(1, half)], pool.at[part_of(2, half)], back))
    for part, forth, back in ((0, ahead, behind), (1, above, below)):
        pool, rim = pools[part], rims[part]
        edge_forward[part].wait_recv()
        relays.append(send(rim.at[part_of(3, 0)], rim.at[part_of(2, 0)], forth))
        edge_backward[part].wait_recv()
        relays.append(send(rim.at[part_of(1, half)], rim.at[part_of(2, half)], back))
    for copy in spread_sums:
        copy.wait_recv()

    span = cosines.shape[1]
    along = lax.broadcasted_iota(jnp.int32, (MOST, span), 1)
    turn = turns_of(sums, list_ref[:, 0:1], list_ref[:, 1:2])
    folded = list_ref[:, 2:3] + along
    folded = jnp.where(folded >= phase_modulus, folded - phase_modulus, folded)
    square = folded * folded
    square = square - phase_modulus * (
        square.astype(jnp.float32) * (1.0 / phase_modulus)
    ).astype(jnp.int32)
    square = jnp.where(square < 0, square + phase_modulus, square)
    square = jnp.where(square >= phase_modulus, square - phase_modulus, square)
    phases = square.astype(jnp.float32) * (2.0 * math.pi / phase_modulus) + (
        list_ref[:, 3:4].astype(jnp.float32) * (math.pi / 4.0) - turn
    )
    cosines[...] = jnp.cos(phases) * scale_ref[:, 0:1]
    sines[...] = jnp.sin(phases) * scale_ref[:, 0:1]

    def spread(ref, j):
        return pltpu.roll(
            jnp.broadcast_to(ref[pl.ds(j, 1), :], (C, span)),
            span - 2 * (C - 1),
            1,
            stride=2,
            stride_axis=0,
        )[:, :X]

    def weigh(pair, carry):
        upper, lower = [], []
        for s in range(2):
            cosine = spread(cosines, 2 * pair + s)
            sine = spread(sines, 2 * pair + s)
            upper += [cosine, -sine]
            lower += [sine, cosine]
        at = pl.ds(pl.multiple_of(pair * 4 * C, 4 * C), 4 * C)
        weights[0:X, at] = jnp.concatenate(upper, axis=0).T.astype(jnp.bfloat16)
        weights[X : 2 * X, at] = jnp.concatenate(lower, axis=0).T.astype(jnp.bfloat16)
        return carry

    lax.fori_loop(0, MOST // 2, weigh, 0)

    for copy in forward[2:] + backward[2:] + relays:
        copy.wait_recv()

    targets = []
    for k in range(1, HOLD):
        for part in range(2):
            d, dc = k // CORES, k % CORES
            to = device(y + d, x, c + dc) if part == 0 else device(y, x + d, c + dc)
            targets.append((part * HOLD + k, to))
    tiles = length // 128

    def cut(q, part, slot):
        local = table[0, part * HOLD * HOLD + slot]
        offset = table[1, part * HOLD * HOLD + slot]
        pool = pools[part]
        back = offset < 0
        rem = jnp.where(back, offset + 128, offset)
        turn = lax.rem(128 - rem, 128)
        keep = lane < 128 - rem
        first = q * wide // 128

        def tile(k):
            if k < 0 or k >= tiles:
                return rims[part][local].astype(jnp.float32)
            return pool[local, :, 128 * k : 128 * (k + 1)].astype(jnp.float32)

        here = tile(first)
        current = pltpu.roll(jnp.where(back, tile(first - 1), here), turn, 1)
        out = []
        for k in range(first, first + wide // 128):
            following_tile = tile(k + 1)
            following = pltpu.roll(jnp.where(back, here, following_tile), turn, 1)
            out.append(jnp.where(keep, current, following).astype(jnp.bfloat16))
            current, here = following, following_tile
        return out

    def build(q):
        for part in range(2):

            def for_self(s, carry):
                for k, value in enumerate(cut(q, part, s)):
                    received[q][part * HOLD * HOLD + s, :, 128 * k : 128 * (k + 1)] = value
                return carry

            def for_others(s, carry):
                for k, value in enumerate(cut(q, part, s)):
                    staging[q % 2, part * HOLD * HOLD + s, :, 128 * k : 128 * (k + 1)] = value
                return carry

            lax.fori_loop(0, HOLD, for_self, 0, unroll=True)
            lax.fori_loop(HOLD, HOLD * HOLD, for_others, 0, unroll=HOLD)

    def ship(q):
        copies = []
        for i, (group, to) in enumerate(targets):
            at = pl.ds(group * HOLD, HOLD)
            copies.append(
                pltpu.make_async_remote_copy(
                    src_ref=staging.at[q % 2, at],
                    dst_ref=received[q].at[at],
                    send_sem=slot_send.at[q, i],
                    recv_sem=slot_recv.at[q, i],
                    device_id={"ping": to},
                    device_id_type=MESH,
                )
            )
            copies[-1].start()
        return copies

    shipped = []
    for q in range(2):
        build(q)
        shipped.append(ship(q))
    rows = X
    for q in range(chunks):
        if q + 2 < chunks:
            for copy in shipped[q]:
                copy.wait_send()
            build(q + 2)
            shipped.append(ship(q + 2))
        for copy in shipped[q]:
            copy.wait_recv()

        def fill(j, carry):
            for part in range(2):
                at = pl.multiple_of(j * 2 * C + part * C, C)
                stacked[pl.ds(at, C), :] = received[q][arrival[part, j]]
            return carry

        lax.fori_loop(0, MOST, fill, 0, unroll=8)
        before[q].wait()

        def multiply(i, carry):
            at = pl.ds(pl.multiple_of(i * rows, rows), rows)
            product = jnp.dot(weights[at, :], stacked[...], preferred_element_type=jnp.float32)
            image[q % 2, at, :] = (image[q % 2, at, :].astype(jnp.float32) + product).astype(
                jnp.bfloat16
            )
            return carry

        lax.fori_loop(0, 2 * X // rows, multiply, 0)
        after[q].start()
        if q >= 1 and q + 1 < chunks:
            after[q - 1].wait()
            before[q + 1].start()
    for copy in started + across + spread_sums + shipped[chunks - 2] + shipped[chunks - 1]:
        copy.wait_send()
    for copy in after[chunks - 2 :]:
        copy.wait()


def focus(table, arrival, echoes, front_pick, rear_pick, entries, scales, earlier, rng_size):
    pings, parts, channels, length = echoes.shape
    owners = SIDE * SIDE * CORES
    chunks = 8
    wide = length // chunks
    slots = 2 * HOLD * HOLD
    count = 2 * (HOLD - 1)
    bf16, f32 = jnp.bfloat16, jnp.float32
    dma = pltpu.SemaphoreType.DMA
    steps = 3 + 8 + 4 + 8
    smem = pl.BlockSpec(memory_space=pltpu.SMEM)
    return pl.pallas_call(
        functools.partial(image_kernel, rng_size),
        out_shape=jax.ShapeDtypeStruct((2 * X, length), bf16),
        in_specs=[smem, smem, ANY, IN_VMEM, IN_VMEM, IN_VMEM, IN_VMEM, ANY],
        out_specs=ANY,
        scratch_shapes=[
            pltpu.VMEM((SIDE * pings, channels, length), bf16),
            pltpu.VMEM((SIDE * pings, channels, length), bf16),
            pltpu.VMEM((SIDE * pings, channels, 128), bf16),
            pltpu.VMEM((SIDE * pings, channels, 128), bf16),
            pltpu.VMEM((parts, channels, length), bf16),
            pltpu.VMEM((2, pings, parts, channels, 128), bf16),
            pltpu.VMEM((rng_size, 8, 128), f32),
            pltpu.VMEM((8, 128), f32),
            pltpu.VMEM((owners, 8, 128), f32),
            pltpu.VMEM((2, slots, channels, wide), bf16),
            pltpu.VMEM((2 * X, MOST * 2 * C), bf16),
            pltpu.VMEM((MOST * 2 * C, wide), bf16),
            pltpu.VMEM((2, 2 * X, wide), bf16),
            pltpu.VMEM((MOST, X + 128), f32),
            pltpu.VMEM((MOST, X + 128), f32),
            dma((2 + 2 * chunks,)),
            dma((steps,)),
            dma((steps,)),
            dma((owners + rng_size,)),
            dma((owners + rng_size,)),
            dma((chunks, count)),
            dma((chunks, count)),
        ]
        + [pltpu.VMEM((slots, channels, wide), bf16)] * chunks,
        compiler_params=pltpu.CompilerParams(
            collective_id=0, has_side_effects=True, vmem_limit_bytes=63 << 20
        ),
        name="focus",
    )(table, arrival, echoes, front_pick, rear_pick, entries, scales, earlier)


def rank_in(groups, positions):
    same = (groups[:, None, :] == groups[:, :, None]) & (positions[None, :] < positions[:, None])[None]
    return jnp.sum(same.astype(jnp.int32), axis=2)


def per_device(echoes, pairing, footprint, counts, offsets, earlier):
    block_len = echoes.shape[3]
    owners = lax.axis_size("ping")
    rng_size = lax.axis_size("rng")
    me = lax.axis_index("ping")
    y, x, c = place(me)

    channel_ids = jnp.arange(C, dtype=jnp.int32)
    front_pick = (pairing[:, 0, :, None] == channel_ids).astype(jnp.bfloat16)
    rear_pick = (pairing[:, 1, :, None] == channel_ids).astype(jnp.bfloat16)

    steps = jnp.arange(HOLD, dtype=jnp.int32)
    tiles = jnp.concatenate(
        [
            device(y + steps // CORES, x, c + steps % CORES),
            device(y, x + steps // CORES, c + steps % CORES),
        ]
    )
    all_tiles = jnp.arange(owners, dtype=jnp.int32)
    chosen = (tiles[:, None] == all_tiles[None, :]).astype(jnp.int32)
    positions = jnp.arange(MOST, dtype=jnp.int32)
    foot = jnp.sum(chosen[:, :, None] * footprint[None], axis=1)
    shift = jnp.sum(chosen[:, :, None] * offsets[None], axis=1)
    count = jnp.sum(chosen * counts[None, :], axis=1)
    listed = positions[None, :] < count[:, None]
    oy, ox, oc = place(foot // PING_DEV)
    by_row = steps[:, None] >= 0
    by_row = jnp.concatenate([by_row, ~by_row], axis=0)
    group = jnp.where(listed, jnp.where(by_row, oy, ox) * CORES + oc, -1)
    rank = rank_in(group, positions)
    here = group == jnp.where(by_row, y, x) * CORES + c
    distance = jnp.where(by_row, ox - x + SIDE, oy - y + SIDE) % SIDE
    source = distance * PING_DEV + foot % PING_DEV
    fits = (here[:, None, :] & (rank[:, None, :] == steps[None, :, None])).astype(jnp.int32)
    table = jnp.stack(
        [
            jnp.sum(fits * source[:, None, :], axis=2).reshape(-1),
            jnp.sum(fits * shift[:, None, :], axis=2).reshape(-1),
        ]
    )
    own_group = jnp.stack([group[0], group[HOLD]])
    own_rank = jnp.stack([rank[0], rank[HOLD]])
    own_place = jnp.stack([y, x])[:, None]
    own_distance = (own_place - own_group // CORES + SIDE) % SIDE
    own_core = (c - own_group % CORES + CORES) % CORES
    arrival = (own_distance * CORES + own_core) * HOLD + own_rank
    arrival = jnp.where(listed[0:1], arrival, arrival[:, 0:1])
    arrival = arrival + jnp.array([[0], [HOLD * HOLD]], jnp.int32)
    entries = jnp.stack(
        [
            foot[0] // PING_DEV,
            foot[0] % PING_DEV,
            jnp.remainder(me * X - foot[0] * SPACING - 2 * (C - 1), phase_modulus),
            shift[0],
        ],
        axis=1,
    )
    scales = listed[0].astype(jnp.float32) / jnp.sqrt(jnp.float32(C) * count[0].astype(jnp.float32))
    image = focus(
        table,
        arrival,
        echoes,
        front_pick,
        rear_pick,
        entries,
        scales[:, None],
        earlier.reshape(2 * X, block_len),
        rng_size,
    )
    return image.reshape(earlier.shape)


def solution(mesh):
    return jax.shard_map(
        per_device,
        mesh=mesh,
        in_specs=(
            P("ping", None, None, "rng"),
            P("ping", None, None),
            P(),
            P(),
            P(),
            P("ping", None, None, "rng"),
        ),
        out_specs=P("ping", None, None, "rng"),
        check_vma=False,
    )
```

```python
import functools
import math

import jax
import jax.numpy as jnp
from jax import lax
from jax.experimental import pallas as pl
from jax.experimental.pallas import tpu as pltpu
from jax.sharding import PartitionSpec as P

C = 32
X = 1024
MOST = 48
PING_DEV = 16
SPACING = X // PING_DEV
SIDE = 4
CORES = 2
HOLD = 8
MESH = pl.DeviceIdType.MESH
ANY = pl.BlockSpec(memory_space=pl.ANY)
IN_VMEM = pl.BlockSpec(memory_space=pltpu.VMEM)

phase_modulus = 4099
small_value = 1e-06


def place(index):
    return index // (SIDE * CORES), (index // CORES) % SIDE, index % CORES


def device(y, x, c):
    return (((y + SIDE) % SIDE) * SIDE + (x + SIDE) % SIDE) * CORES + (c + CORES) % CORES


def turns_of(sums_ref, owner, local):
    sums = sums_ref[:, 0, :]
    owners = sums.shape[0]
    lane = lax.broadcasted_iota(jnp.int32, (owners, 128), 1)
    row = lax.broadcasted_iota(jnp.int32, (owners, 128), 0)
    front = pltpu.roll(sums, 128 - PING_DEV, 1)
    rear = pltpu.roll(sums, 128 - 2 * PING_DEV, 1)
    valid = lane < PING_DEV
    energy = jnp.where(valid, front * rear, 1.0)
    running = jnp.where(valid, sums / (jnp.sqrt(energy) + small_value), 0.0)
    step = 1
    while step < PING_DEV:
        running = running + jnp.where(lane >= step, pltpu.roll(running, step, 1), 0.0)
        step *= 2
    last = jnp.sum(jnp.where(lane == PING_DEV - 1, running, 0.0), axis=1, keepdims=True)
    before = jnp.broadcast_to(last, (owners, 128))
    step = 1
    while step < owners:
        before = before + jnp.where(row >= step, pltpu.roll(before, step, 0), 0.0)
        step *= 2
    before = jnp.where(row >= 1, pltpu.roll(before, 1, 0), 0.0)
    turn = jnp.where(valid, running + before, 0.0)
    entries = owner.shape[0]
    lane = lax.broadcasted_iota(jnp.int32, (entries, 128), 1)
    at_lane = lane == local
    picked = jnp.zeros((entries, 128), jnp.float32)
    for k in range(owners):
        picked = picked + jnp.where(at_lane & (owner == k), turn[k : k + 1, :], 0.0)
    return jnp.sum(picked, axis=1, keepdims=True)


def image_kernel(
    rng_size,
    table,
    arrival,
    echo_ref,
    front_ref,
    rear_ref,
    list_ref,
    scale_ref,
    earlier_ref,
    out_ref,
    row_first,
    row_second,
    column_first,
    column_second,
    row_low,
    row_high,
    column_low,
    column_high,
    lead,
    partial,
    total,
    sums,
    staging,
    weights,
    stacked,
    image,
    cosines,
    sines,
    local_sem,
    send_sem,
    recv_sem,
    sum_send,
    sum_recv,
    slot_send,
    slot_recv,
    edge_send,
    edge_recv,
    *received,
):
    me = lax.axis_index("ping")
    level = lax.axis_index("rng")
    y, x, c = place(me)
    owners = SIDE * SIDE * CORES
    pings, half = PING_DEV, PING_DEV // 2
    length = echo_ref.shape[3]
    chunks, wide = len(received), stacked.shape[1]
    order = [1, 2, 4, 5, 6, 3, 0, 7]

    barrier = pltpu.get_barrier_semaphore()
    for step in range(1, owners):
        pl.semaphore_signal(
            barrier, inc=1, device_id={"ping": (me + step) % owners}, device_id_type=MESH
        )
    for step in range(1, rng_size):
        pl.semaphore_signal(
            barrier, inc=1, device_id={"rng": (level + step) % rng_size}, device_id_type=MESH
        )
    pools = ((row_first, row_second), (column_first, column_second))
    lows, highs = (row_low, column_low), (row_high, column_high)
    span = length // 2
    spans = (pl.ds(0, span), pl.ds(span, span))
    own = [
        pltpu.make_async_copy(
            echo_ref.at[:, part, :, spans[h]],
            pools[part][h].at[pl.ds(0, pings)],
            local_sem.at[2 * chunks + 2 * part + h],
        )
        for part in range(2)
        for h in range(2)
    ]
    before = [
        pltpu.make_async_copy(
            earlier_ref.at[:, pl.ds(order[q] * wide, wide)], image.at[q % 2], local_sem.at[q]
        )
        for q in range(chunks)
    ]
    after = [
        pltpu.make_async_copy(
            image.at[q % 2], out_ref.at[:, pl.ds(order[q] * wide, wide)], local_sem.at[chunks + q]
        )
        for q in range(chunks)
    ]
    for copy in own + before[:2]:
        copy.start()
    pl.semaphore_wait(barrier, owners + rng_size - 2)

    started = []

    def send(src, dst, target):
        i = len(started)
        copy = pltpu.make_async_remote_copy(
            src_ref=src,
            dst_ref=dst,
            send_sem=send_sem.at[i],
            recv_sem=recv_sem.at[i],
            device_id=target,
            device_id_type=MESH,
        )
        copy.start()
        started.append(copy)
        return copy

    up, down = {"rng": (level + 1) % rng_size}, {"rng": (level + rng_size - 1) % rng_size}
    ahead = {"ping": device(y, x + 1, c)}
    behind = {"ping": device(y, x - 1, c)}
    above = {"ping": device(y + 1, x, c)}
    below = {"ping": device(y - 1, x, c)}
    low, high = pl.ds(0, half), pl.ds(half, half)

    def part_of(distance, start):
        return pl.ds(distance * pings + start, half)

    from_lead = send(echo_ref.at[pings - 1], lead, {"ping": (me + 1) % owners})

    edge_copies = []

    def send_edges(sources_low, sources_high, at):
        for part in range(2):
            for source, pool, target in (
                (sources_low[part], lows[part], up),
                (sources_high[part], highs[part], down),
            ):
                i = len(edge_copies)
                edge_copies.append(
                    pltpu.make_async_remote_copy(
                        src_ref=source,
                        dst_ref=pool.at[at],
                        send_sem=edge_send.at[i],
                        recv_sem=edge_recv.at[i],
                        device_id=target,
                        device_id_type=MESH,
                    )
                )
                edge_copies[-1].start()

    def send_gathered_edges(distance):
        at = pl.ds(distance * pings, pings)
        send_edges(
            [pools[part][1].at[at, :, pl.ds(span - 128, 128)] for part in range(2)],
            [pools[part][0].at[at, :, pl.ds(0, 128)] for part in range(2)],
            at,
        )

    send_edges(
        [echo_ref.at[:, part, :, pl.ds(length - 128, 128)] for part in range(2)],
        [echo_ref.at[:, part, :, pl.ds(0, 128)] for part in range(2)],
        pl.ds(0, pings),
    )
    ways = ((0, ahead, behind), (1, above, below))
    forward, backward = [[], []], [[], []]
    for h in range(2):
        for turn in range(2):
            for part, forth, back in ways:
                first, second = (low, high) if turn == 0 else (high, low)
                pool = pools[part][h]
                forward[h].append(
                    send(
                        echo_ref.at[first, part, :, spans[h]], pool.at[part_of(3, turn * half)], forth
                    )
                )
                backward[h].append(
                    send(
                        echo_ref.at[second, part, :, spans[h]],
                        pool.at[part_of(1, (1 - turn) * half)],
                        back,
                    )
                )

    lane = lax.broadcasted_iota(jnp.int32, (C, 128), 1)
    use_low = level > 0
    use_high = level < rng_size - 1

    for copy in own:
        copy.wait()
    from_lead.wait_recv()
    place_lane = lax.broadcasted_iota(jnp.int32, (1, 128), 1)

    def fold(value):
        out = value[:, 0:128]
        for k in range(1, span // 128):
            out = out + value[:, 128 * k : 128 * (k + 1)]
        out = jnp.sum(out, axis=0, keepdims=True)
        return jnp.sum(out, axis=1, keepdims=True)

    def correlate(p, front_source, acc):
        front, rear = front_ref[p], rear_ref[p]
        dot = functools.partial(jnp.dot, preferred_element_type=jnp.float32)
        cross = front_energy = rear_energy = 0.0
        for h in range(2):
            front_real = dot(front, front_source(0, h))
            front_imag = dot(front, front_source(1, h))
            rear_real = dot(rear, pools[0][h][p])
            rear_imag = dot(rear, pools[1][h][p])
            cross = cross + fold(front_real * rear_imag - front_imag * rear_real)
            front_energy = front_energy + fold(front_real * front_real + front_imag * front_imag)
            rear_energy = rear_energy + fold(rear_real * rear_real + rear_imag * rear_imag)
        acc = jnp.where(place_lane == p, cross, acc)
        acc = jnp.where(place_lane == p + pings, front_energy, acc)
        return jnp.where(place_lane == p + 2 * pings, rear_energy, acc)

    mine = correlate(
        0, lambda part, h: lead[part, :, span * h : span * (h + 1)], jnp.zeros((1, 128), jnp.float32)
    )
    mine = jnp.where((me == 0) & (place_lane < 2 * pings), 0.0, mine)
    mine = lax.fori_loop(
        1, pings, lambda p, acc: correlate(p, lambda part, h: pools[part][h][p - 1], acc), mine
    )
    partial[0] = mine

    across = []
    for step in range(1, rng_size):
        across.append(
            pltpu.make_async_remote_copy(
                src_ref=partial.at[0],
                dst_ref=partial.at[step],
                send_sem=sum_send.at[owners + step],
                recv_sem=sum_recv.at[owners + step],
                device_id={"rng": (level + step) % rng_size},
                device_id_type=MESH,
            )
        )
        across[-1].start()
    for copy in across:
        copy.wait_recv()
    whole = mine
    for step in range(1, rng_size):
        whole = whole + partial[step]
    total[...] = whole
    sums[me] = whole
    spread_sums = []
    for step in range(1, owners):
        spread_sums.append(
            pltpu.make_async_remote_copy(
                src_ref=total,
                dst_ref=sums.at[me],
                send_sem=sum_send.at[step],
                recv_sem=sum_recv.at[step],
                device_id={"ping": (me + step) % owners},
                device_id_type=MESH,
            )
        )
        spread_sums[-1].start()

    relays = [[], []]
    for h in range(2):
        for part, forth, back in ways:
            pool = pools[part][h]
            forward[h][part].wait_recv()
            relays[h].append(send(pool.at[part_of(3, 0)], pool.at[part_of(2, 0)], forth))
            backward[h][part].wait_recv()
            relays[h].append(send(pool.at[part_of(1, half)], pool.at[part_of(2, half)], back))
    for copy in spread_sums:
        copy.wait_recv()

    chirp = cosines.shape[1]
    along = lax.broadcasted_iota(jnp.int32, (MOST, chirp), 1)
    turn = turns_of(sums, list_ref[:, 0:1], list_ref[:, 1:2])
    folded = list_ref[:, 2:3] + along
    folded = jnp.where(folded >= phase_modulus, folded - phase_modulus, folded)
    square = folded * folded
    square = square - phase_modulus * (
        square.astype(jnp.float32) * (1.0 / phase_modulus)
    ).astype(jnp.int32)
    square = jnp.where(square < 0, square + phase_modulus, square)
    square = jnp.where(square >= phase_modulus, square - phase_modulus, square)
    phases = square.astype(jnp.float32) * (2.0 * math.pi / phase_modulus) + (
        list_ref[:, 3:4].astype(jnp.float32) * (math.pi / 4.0) - turn
    )
    cosines[...] = jnp.cos(phases) * scale_ref[:, 0:1]
    sines[...] = jnp.sin(phases) * scale_ref[:, 0:1]

    def spread(ref, j):
        return pltpu.roll(
            jnp.broadcast_to(ref[pl.ds(j, 1), :], (C, chirp)),
            chirp - 2 * (C - 1),
            1,
            stride=2,
            stride_axis=0,
        )[:, :X]

    def weigh(pair, carry):
        upper, lower = [], []
        for s in range(2):
            cosine = spread(cosines, 2 * pair + s)
            sine = spread(sines, 2 * pair + s)
            upper += [cosine, -sine]
            lower += [sine, cosine]
        at = pl.ds(pl.multiple_of(pair * 4 * C, 4 * C), 4 * C)
        weights[0:X, at] = jnp.concatenate(upper, axis=0).T.astype(jnp.bfloat16)
        weights[X : 2 * X, at] = jnp.concatenate(lower, axis=0).T.astype(jnp.bfloat16)
        return carry

    lax.fori_loop(0, MOST // 2, weigh, 0)

    for copy in forward[0][2:] + backward[0][2:] + relays[0]:
        copy.wait_recv()

    targets = []
    for k in range(1, HOLD):
        for part in range(2):
            d, dc = k // CORES, k % CORES
            to = device(y + d, x, c + dc) if part == 0 else device(y, x + d, c + dc)
            targets.append((part * HOLD + k, to))
    tiles = length // 128

    def cut(q, part, slot):
        local = table[0, part * HOLD * HOLD + slot]
        offset = table[1, part * HOLD * HOLD + slot]
        back = offset < 0
        rem = jnp.where(back, offset + 128, offset)
        turn = lax.rem(128 - rem, 128)
        keep = lane < 128 - rem
        first = q * wide // 128

        def tile(k):
            if k < 0:
                return jnp.where(use_low, lows[part][local].astype(jnp.float32), 0.0)
            if k >= tiles:
                return jnp.where(use_high, highs[part][local].astype(jnp.float32), 0.0)
            at = 128 * k % span
            return pools[part][128 * k // span][local, :, at : at + 128].astype(jnp.float32)

        here = tile(first)
        current = pltpu.roll(jnp.where(back, tile(first - 1), here), turn, 1)
        out = []
        for k in range(first, first + wide // 128):
            following_tile = tile(k + 1)
            following = pltpu.roll(jnp.where(back, here, following_tile), turn, 1)
            out.append(jnp.where(keep, current, following).astype(jnp.bfloat16))
            current, here = following, following_tile
        return out

    def build(i):
        q = order[i]
        for part in range(2):

            def for_self(s, carry):
                for k, value in enumerate(cut(q, part, s)):
                    received[i][part * HOLD * HOLD + s, :, 128 * k : 128 * (k + 1)] = value
                return carry

            def for_others(s, carry):
                for k, value in enumerate(cut(q, part, s)):
                    staging[i % 2, part * HOLD * HOLD + s, :, 128 * k : 128 * (k + 1)] = value
                return carry

            lax.fori_loop(0, HOLD, for_self, 0, unroll=True)
            lax.fori_loop(HOLD, HOLD * HOLD, for_others, 0, unroll=HOLD)

    def ship(i):
        copies = []
        for k, (group, to) in enumerate(targets):
            at = pl.ds(group * HOLD, HOLD)
            copies.append(
                pltpu.make_async_remote_copy(
                    src_ref=staging.at[i % 2, at],
                    dst_ref=received[i].at[at],
                    send_sem=slot_send.at[i, k],
                    recv_sem=slot_recv.at[i, k],
                    device_id={"ping": to},
                    device_id_type=MESH,
                )
            )
            copies[-1].start()
        return copies

    shipped = []
    for i in range(2):
        build(i)
        shipped.append(ship(i))
    for copy in forward[1][2:] + backward[1][2:] + relays[1]:
        copy.wait_recv()
    for distance in range(1, SIDE):
        send_gathered_edges(distance)
    rows = X
    for i in range(chunks):
        if i + 2 < chunks:
            for copy in shipped[i]:
                copy.wait_send()
            if i + 2 == order.index(0):
                for copy in edge_copies:
                    copy.wait_recv()
            build(i + 2)
            shipped.append(ship(i + 2))
        for copy in shipped[i]:
            copy.wait_recv()

        def fill(j, carry):
            for part in range(2):
                at = pl.multiple_of(j * 2 * C + part * C, C)
                stacked[pl.ds(at, C), :] = received[i][arrival[part, j]]
            return carry

        lax.fori_loop(0, MOST, fill, 0, unroll=8)
        before[i].wait()

        def multiply(k, carry):
            at = pl.ds(pl.multiple_of(k * rows, rows), rows)
            product = jnp.dot(weights[at, :], stacked[...], preferred_element_type=jnp.float32)
            image[i % 2, at, :] = (image[i % 2, at, :].astype(jnp.float32) + product).astype(
                jnp.bfloat16
            )
            return carry

        lax.fori_loop(0, 2 * X // rows, multiply, 0)
        after[i].start()
        if i >= 1 and i + 1 < chunks:
            after[i - 1].wait()
            before[i + 1].start()
    for copy in started + across + edge_copies + spread_sums + shipped[chunks - 2] + shipped[chunks - 1]:
        copy.wait_send()
    for copy in after[chunks - 2 :]:
        copy.wait()


def focus(table, arrival, echoes, front_pick, rear_pick, entries, scales, earlier, rng_size):
    pings, parts, channels, length = echoes.shape
    owners = SIDE * SIDE * CORES
    chunks = 8
    wide = length // chunks
    slots = 2 * HOLD * HOLD
    count = 2 * (HOLD - 1)
    bf16, f32 = jnp.bfloat16, jnp.float32
    dma = pltpu.SemaphoreType.DMA
    steps = 1 + 16 + 8
    smem = pl.BlockSpec(memory_space=pltpu.SMEM)
    return pl.pallas_call(
        functools.partial(image_kernel, rng_size),
        out_shape=jax.ShapeDtypeStruct((2 * X, length), bf16),
        in_specs=[smem, smem, ANY, IN_VMEM, IN_VMEM, IN_VMEM, IN_VMEM, ANY],
        out_specs=ANY,
        scratch_shapes=[
            *[pltpu.VMEM((SIDE * pings, channels, length // 2), bf16)] * 4,
            *[pltpu.VMEM((SIDE * pings, channels, 128), bf16)] * 4,
            pltpu.VMEM((parts, channels, length), bf16),
            pltpu.VMEM((rng_size, 1, 128), f32),
            pltpu.VMEM((1, 128), f32),
            pltpu.VMEM((owners, 1, 128), f32),
            pltpu.VMEM((2, slots, channels, wide), bf16),
            pltpu.VMEM((2 * X, MOST * 2 * C), bf16),
            pltpu.VMEM((MOST * 2 * C, wide), bf16),
            pltpu.VMEM((2, 2 * X, wide), bf16),
            pltpu.VMEM((MOST, X + 128), f32),
            pltpu.VMEM((MOST, X + 128), f32),
            dma((4 + 2 * chunks,)),
            dma((steps,)),
            dma((steps,)),
            dma((owners + rng_size,)),
            dma((owners + rng_size,)),
            dma((chunks, count)),
            dma((chunks, count)),
            dma((4 * SIDE,)),
            dma((4 * SIDE,)),
        ]
        + [pltpu.VMEM((slots, channels, wide), bf16)] * chunks,
        compiler_params=pltpu.CompilerParams(
            collective_id=0, has_side_effects=True, vmem_limit_bytes=63 << 20
        ),
        name="focus",
    )(table, arrival, echoes, front_pick, rear_pick, entries, scales, earlier)


def move_kernel(source, target, held, load_sem, store_sem):
    pieces = load_sem.shape[0]
    rows = held.shape[0] // pieces
    loads, stores = [], []
    for i in range(pieces):
        at = pl.ds(rows * i, rows)
        loads.append(pltpu.make_async_copy(source.at[at], held.at[at], load_sem.at[i]))
        stores.append(pltpu.make_async_copy(held.at[at], target.at[at], store_sem.at[i]))
        loads[-1].start()
    for load, store in zip(loads, stores):
        load.wait()
        store.start()
    for store in stores:
        store.wait()


def move(image):
    return pl.pallas_call(
        move_kernel,
        out_shape=jax.ShapeDtypeStruct(image.shape, image.dtype),
        in_specs=[ANY],
        out_specs=ANY,
        scratch_shapes=[
            pltpu.VMEM(image.shape, image.dtype),
            pltpu.SemaphoreType.DMA((8,)),
            pltpu.SemaphoreType.DMA((8,)),
        ],
        name="move",
    )(image)


def rank_in(groups, positions):
    same = (groups[:, None, :] == groups[:, :, None]) & (positions[None, :] < positions[:, None])[None]
    return jnp.sum(same.astype(jnp.int32), axis=2)


def per_device(echoes, pairing, footprint, counts, offsets, earlier):
    block_len = echoes.shape[3]
    owners = lax.axis_size("ping")
    rng_size = lax.axis_size("rng")
    me = lax.axis_index("ping")
    y, x, c = place(me)

    channel_ids = jnp.arange(C, dtype=jnp.int32)
    front_pick = (pairing[:, 0, :, None] == channel_ids).astype(jnp.bfloat16)
    rear_pick = (pairing[:, 1, :, None] == channel_ids).astype(jnp.bfloat16)

    steps = jnp.arange(HOLD, dtype=jnp.int32)
    tiles = jnp.concatenate(
        [
            device(y + steps // CORES, x, c + steps % CORES),
            device(y, x + steps // CORES, c + steps % CORES),
        ]
    )
    all_tiles = jnp.arange(owners, dtype=jnp.int32)
    chosen = (tiles[:, None] == all_tiles[None, :]).astype(jnp.int32)
    positions = jnp.arange(MOST, dtype=jnp.int32)
    foot = jnp.sum(chosen[:, :, None] * footprint[None], axis=1)
    shift = jnp.sum(chosen[:, :, None] * offsets[None], axis=1)
    count = jnp.sum(chosen * counts[None, :], axis=1)
    listed = positions[None, :] < count[:, None]
    oy, ox, oc = place(foot // PING_DEV)
    by_row = steps[:, None] >= 0
    by_row = jnp.concatenate([by_row, ~by_row], axis=0)
    group = jnp.where(listed, jnp.where(by_row, oy, ox) * CORES + oc, -1)
    rank = rank_in(group, positions)
    here = group == jnp.where(by_row, y, x) * CORES + c
    distance = jnp.where(by_row, ox - x + SIDE, oy - y + SIDE) % SIDE
    source = distance * PING_DEV + foot % PING_DEV
    fits = (here[:, None, :] & (rank[:, None, :] == steps[None, :, None])).astype(jnp.int32)
    table = jnp.stack(
        [
            jnp.sum(fits * source[:, None, :], axis=2).reshape(-1),
            jnp.sum(fits * shift[:, None, :], axis=2).reshape(-1),
        ]
    )
    own_group = jnp.stack([group[0], group[HOLD]])
    own_rank = jnp.stack([rank[0], rank[HOLD]])
    own_place = jnp.stack([y, x])[:, None]
    own_distance = (own_place - own_group // CORES + SIDE) % SIDE
    own_core = (c - own_group % CORES + CORES) % CORES
    arrival = (own_distance * CORES + own_core) * HOLD + own_rank
    arrival = jnp.where(listed[0:1], arrival, arrival[:, 0:1])
    arrival = arrival + jnp.array([[0], [HOLD * HOLD]], jnp.int32)
    entries = jnp.stack(
        [
            foot[0] // PING_DEV,
            foot[0] % PING_DEV,
            jnp.remainder(me * X - foot[0] * SPACING - 2 * (C - 1), phase_modulus),
            shift[0],
        ],
        axis=1,
    )
    scales = listed[0].astype(jnp.float32) / jnp.sqrt(jnp.float32(C) * count[0].astype(jnp.float32))
    image = focus(
        table,
        arrival,
        echoes,
        front_pick,
        rear_pick,
        entries,
        scales[:, None],
        earlier.reshape(2 * X, block_len),
        rng_size,
    )
    return move(image).reshape(earlier.shape)


def solution(mesh):
    return jax.shard_map(
        per_device,
        mesh=mesh,
        in_specs=(
            P("ping", None, None, "rng"),
            P("ping", None, None),
            P(),
            P(),
            P(),
            P("ping", None, None, "rng"),
        ),
        out_specs=P("ping", None, None, "rng"),
        check_vma=False,
    )
```

```python
import functools
import math

import jax
import jax.numpy as jnp
from jax import lax
from jax.experimental import pallas as pl
from jax.experimental.pallas import tpu as pltpu
from jax.sharding import PartitionSpec as P

C = 32
X = 1024
MOST = 48
PING_DEV = 16
SPACING = X // PING_DEV
SIDE = 4
CORES = 2
HOLD = 8
MESH = pl.DeviceIdType.MESH
ANY = pl.BlockSpec(memory_space=pl.ANY)

phase_modulus = 4099
small_value = 1e-06


def place(index):
    return index // (SIDE * CORES), (index // CORES) % SIDE, index % CORES


def device(y, x, c):
    return (((y + SIDE) % SIDE) * SIDE + (x + SIDE) % SIDE) * CORES + (c + CORES) % CORES


def turns_of(sums_ref, owner, local):
    sums = sums_ref[:, 0, :]
    owners = sums.shape[0]
    lane = lax.broadcasted_iota(jnp.int32, (owners, 128), 1)
    row = lax.broadcasted_iota(jnp.int32, (owners, 128), 0)
    front = pltpu.roll(sums, 128 - PING_DEV, 1)
    rear = pltpu.roll(sums, 128 - 2 * PING_DEV, 1)
    valid = lane < PING_DEV
    energy = jnp.where(valid, front * rear, 1.0)
    running = jnp.where(valid, sums / (jnp.sqrt(energy) + small_value), 0.0)
    step = 1
    while step < PING_DEV:
        running = running + jnp.where(lane >= step, pltpu.roll(running, step, 1), 0.0)
        step *= 2
    last = jnp.sum(jnp.where(lane == PING_DEV - 1, running, 0.0), axis=1, keepdims=True)
    before = jnp.broadcast_to(last, (owners, 128))
    step = 1
    while step < owners:
        before = before + jnp.where(row >= step, pltpu.roll(before, step, 0), 0.0)
        step *= 2
    before = jnp.where(row >= 1, pltpu.roll(before, 1, 0), 0.0)
    turn = jnp.where(valid, running + before, 0.0)
    entries = owner.shape[0]
    lane = lax.broadcasted_iota(jnp.int32, (entries, 128), 1)
    at_lane = lane == local
    picked = jnp.zeros((entries, 128), jnp.float32)
    for k in range(owners):
        picked = picked + jnp.where(at_lane & (owner == k), turn[k : k + 1, :], 0.0)
    return jnp.sum(picked, axis=1, keepdims=True)


def image_kernel(
    rng_size,
    footprint,
    counts,
    offsets,
    pairing,
    echo_ref,
    earlier_ref,
    out_ref,
    table,
    arrival,
    row_first,
    row_second,
    column_first,
    column_second,
    row_low,
    row_high,
    column_low,
    column_high,
    lead,
    partial,
    total,
    sums,
    staging,
    weights,
    stacked,
    image,
    cosines,
    sines,
    local_sem,
    send_sem,
    recv_sem,
    sum_send,
    sum_recv,
    slot_send,
    slot_recv,
    edge_send,
    edge_recv,
    *received,
):
    me = lax.axis_index("ping")
    level = lax.axis_index("rng")
    y, x, c = place(me)
    owners = SIDE * SIDE * CORES
    pings, half = PING_DEV, PING_DEV // 2
    length = echo_ref.shape[3]
    chunks, wide = len(received), stacked.shape[1]
    order = [1, 2, 4, 5, 6, 3, 0, 7]

    barrier = pltpu.get_barrier_semaphore()
    for step in range(1, owners):
        pl.semaphore_signal(
            barrier, inc=1, device_id={"ping": (me + step) % owners}, device_id_type=MESH
        )
    for step in range(1, rng_size):
        pl.semaphore_signal(
            barrier, inc=1, device_id={"rng": (level + step) % rng_size}, device_id_type=MESH
        )
    pools = ((row_first, row_second), (column_first, column_second))
    lows, highs = (row_low, column_low), (row_high, column_high)
    span = length // 2
    spans = (pl.ds(0, span), pl.ds(span, span))
    own = [
        pltpu.make_async_copy(
            echo_ref.at[:, part, :, spans[h]],
            pools[part][h].at[pl.ds(0, pings)],
            local_sem.at[2 * chunks + 2 * part + h],
        )
        for part in range(2)
        for h in range(2)
    ]
    before = [
        pltpu.make_async_copy(
            earlier_ref.at[:, pl.ds(order[q] * wide, wide)], image.at[q % 2], local_sem.at[q]
        )
        for q in range(chunks)
    ]
    after = [
        pltpu.make_async_copy(
            image.at[q % 2], out_ref.at[:, pl.ds(order[q] * wide, wide)], local_sem.at[chunks + q]
        )
        for q in range(chunks)
    ]
    for copy in own + before[:2]:
        copy.start()
    pl.semaphore_wait(barrier, owners + rng_size - 2)

    started = []

    def send(src, dst, target):
        i = len(started)
        copy = pltpu.make_async_remote_copy(
            src_ref=src,
            dst_ref=dst,
            send_sem=send_sem.at[i],
            recv_sem=recv_sem.at[i],
            device_id=target,
            device_id_type=MESH,
        )
        copy.start()
        started.append(copy)
        return copy

    up, down = {"rng": (level + 1) % rng_size}, {"rng": (level + rng_size - 1) % rng_size}
    ahead = {"ping": device(y, x + 1, c)}
    behind = {"ping": device(y, x - 1, c)}
    above = {"ping": device(y + 1, x, c)}
    below = {"ping": device(y - 1, x, c)}
    low, high = pl.ds(0, half), pl.ds(half, half)

    def part_of(distance, start):
        return pl.ds(distance * pings + start, half)

    from_lead = send(echo_ref.at[pings - 1], lead, {"ping": (me + 1) % owners})

    edge_copies = []

    def send_edges(sources_low, sources_high, at):
        for part in range(2):
            for source, pool, target in (
                (sources_low[part], lows[part], up),
                (sources_high[part], highs[part], down),
            ):
                i = len(edge_copies)
                edge_copies.append(
                    pltpu.make_async_remote_copy(
                        src_ref=source,
                        dst_ref=pool.at[at],
                        send_sem=edge_send.at[i],
                        recv_sem=edge_recv.at[i],
                        device_id=target,
                        device_id_type=MESH,
                    )
                )
                edge_copies[-1].start()

    def send_gathered_edges(distance):
        at = pl.ds(distance * pings, pings)
        send_edges(
            [pools[part][1].at[at, :, pl.ds(span - 128, 128)] for part in range(2)],
            [pools[part][0].at[at, :, pl.ds(0, 128)] for part in range(2)],
            at,
        )

    send_edges(
        [echo_ref.at[:, part, :, pl.ds(length - 128, 128)] for part in range(2)],
        [echo_ref.at[:, part, :, pl.ds(0, 128)] for part in range(2)],
        pl.ds(0, pings),
    )
    ways = ((0, ahead, behind), (1, above, below))
    forward, backward = [[], []], [[], []]
    for h in range(2):
        for turn in range(2):
            for part, forth, back in ways:
                first, second = (low, high) if turn == 0 else (high, low)
                pool = pools[part][h]
                forward[h].append(
                    send(
                        echo_ref.at[first, part, :, spans[h]], pool.at[part_of(3, turn * half)], forth
                    )
                )
                backward[h].append(
                    send(
                        echo_ref.at[second, part, :, spans[h]],
                        pool.at[part_of(1, (1 - turn) * half)],
                        back,
                    )
                )

    lane = lax.broadcasted_iota(jnp.int32, (C, 128), 1)
    use_low = level > 0
    use_high = level < rng_size - 1

    def owner_of(ping):
        owner = ping >> 4
        return owner >> 3, (owner >> 1) & (SIDE - 1), owner & (CORES - 1)

    for part in range(2):
        for k in range(HOLD):
            d, dc = k // CORES, k % CORES
            tile_id = device(y + d, x, c + dc) if part == 0 else device(y, x + d, c + dc)
            limit = counts[tile_id]

            def scan(j, carry, part=part, tile_id=tile_id, limit=limit):
                filled, sources, shifts = carry
                ping = footprint[tile_id, j]
                oy, ox, oc = owner_of(ping)
                near = oy == y if part == 0 else ox == x
                match = near & (oc == c) & (j < limit)
                away = (ox - x if part == 0 else oy - y) + SIDE
                source = (away & (SIDE - 1)) * PING_DEV + (ping & (PING_DEV - 1))
                shift = offsets[tile_id, j]
                at = jnp.where(match, filled, -1)
                sources = tuple(jnp.where(at == i, source, v) for i, v in enumerate(sources))
                shifts = tuple(jnp.where(at == i, shift, v) for i, v in enumerate(shifts))
                return filled + match.astype(jnp.int32), sources, shifts

            zeros = (jnp.int32(0),) * HOLD
            _, sources, shifts = lax.fori_loop(0, MOST, scan, (jnp.int32(0), zeros, zeros))
            for i in range(HOLD):
                table[0, (part * HOLD + k) * HOLD + i] = sources[i]
                table[1, (part * HOLD + k) * HOLD + i] = shifts[i]

    own_limit = counts[me]
    for part in range(2):

        def scan_own(j, carry, part=part):
            first, held = carry
            oy, ox, oc = owner_of(footprint[me, j])
            at = oy if part == 0 else ox
            group = at * CORES + oc
            rank = jnp.int32(0)
            for g in range(HOLD):
                rank = jnp.where(group == g, held[g], rank)
            away = ((y if part == 0 else x) - at + SIDE) & (SIDE - 1)
            core = (c - oc + CORES) & (CORES - 1)
            slot = ((part * SIDE + away) * CORES + core) * HOLD + rank
            first = jnp.where(j == 0, slot, first)
            listed = j < own_limit
            arrival[part, j] = jnp.where(listed, slot, first)
            entered = jnp.where(listed, group, -1)
            held = tuple(v + jnp.where(entered == g, 1, 0) for g, v in enumerate(held))
            return first, held

        lax.fori_loop(0, MOST, scan_own, (jnp.int32(0), (jnp.int32(0),) * HOLD))

    for copy in own:
        copy.wait()
    from_lead.wait_recv()
    place_lane = lax.broadcasted_iota(jnp.int32, (1, 128), 1)

    def fold(value):
        out = value[:, 0:128]
        for k in range(1, span // 128):
            out = out + value[:, 128 * k : 128 * (k + 1)]
        out = jnp.sum(out, axis=0, keepdims=True)
        return jnp.sum(out, axis=1, keepdims=True)

    pair_row = lax.broadcasted_iota(jnp.int32, (8, C), 0)
    channel = lax.broadcasted_iota(jnp.int32, (8, C), 1)

    def picks(p, side):
        wanted = jnp.zeros((8, C), jnp.int32)
        for k in range(8):
            wanted = jnp.where(pair_row == k, pairing[p, side, k], wanted)
        return jnp.where(channel == wanted, 1.0, 0.0).astype(jnp.bfloat16)

    def correlate(p, front_source, acc):
        front, rear = picks(p, 0), picks(p, 1)
        dot = functools.partial(jnp.dot, preferred_element_type=jnp.float32)
        cross = front_energy = rear_energy = 0.0
        for h in range(2):
            front_real = dot(front, front_source(0, h))
            front_imag = dot(front, front_source(1, h))
            rear_real = dot(rear, pools[0][h][p])
            rear_imag = dot(rear, pools[1][h][p])
            cross = cross + fold(front_real * rear_imag - front_imag * rear_real)
            front_energy = front_energy + fold(front_real * front_real + front_imag * front_imag)
            rear_energy = rear_energy + fold(rear_real * rear_real + rear_imag * rear_imag)
        acc = jnp.where(place_lane == p, cross, acc)
        acc = jnp.where(place_lane == p + pings, front_energy, acc)
        return jnp.where(place_lane == p + 2 * pings, rear_energy, acc)

    mine = correlate(
        0, lambda part, h: lead[part, :, span * h : span * (h + 1)], jnp.zeros((1, 128), jnp.float32)
    )
    mine = jnp.where((me == 0) & (place_lane < 2 * pings), 0.0, mine)
    mine = lax.fori_loop(
        1, pings, lambda p, acc: correlate(p, lambda part, h: pools[part][h][p - 1], acc), mine
    )
    partial[0] = mine

    across = []
    for step in range(1, rng_size):
        across.append(
            pltpu.make_async_remote_copy(
                src_ref=partial.at[0],
                dst_ref=partial.at[step],
                send_sem=sum_send.at[owners + step],
                recv_sem=sum_recv.at[owners + step],
                device_id={"rng": (level + step) % rng_size},
                device_id_type=MESH,
            )
        )
        across[-1].start()
    for copy in across:
        copy.wait_recv()
    whole = mine
    for step in range(1, rng_size):
        whole = whole + partial[step]
    total[...] = whole
    sums[me] = whole
    spread_sums = []
    for step in range(1, owners):
        spread_sums.append(
            pltpu.make_async_remote_copy(
                src_ref=total,
                dst_ref=sums.at[me],
                send_sem=sum_send.at[step],
                recv_sem=sum_recv.at[step],
                device_id={"ping": (me + step) % owners},
                device_id_type=MESH,
            )
        )
        spread_sums[-1].start()

    relays = [[], []]
    for h in range(2):
        for part, forth, back in ways:
            pool = pools[part][h]
            forward[h][part].wait_recv()
            relays[h].append(send(pool.at[part_of(3, 0)], pool.at[part_of(2, 0)], forth))
            backward[h][part].wait_recv()
            relays[h].append(send(pool.at[part_of(1, half)], pool.at[part_of(2, half)], back))
    for copy in spread_sums:
        copy.wait_recv()

    chirp = cosines.shape[1]
    entry = lax.broadcasted_iota(jnp.int32, (MOST, 128), 0)
    foot = jnp.zeros((MOST, 128), jnp.int32)
    shift = jnp.zeros((MOST, 128), jnp.int32)
    for j in range(MOST):
        foot = jnp.where(entry == j, footprint[me, j], foot)
        shift = jnp.where(entry == j, offsets[me, j], shift)
    listed = jnp.where(entry < own_limit, 1.0, 0.0)
    channels = jnp.full((MOST, 128), own_limit, jnp.int32).astype(jnp.float32) * jnp.float32(C)
    scale = (listed / jnp.sqrt(channels))[:, 0:1]

    def modulo(value):
        value = value - phase_modulus * (
            value.astype(jnp.float32) * (1.0 / phase_modulus)
        ).astype(jnp.int32)
        value = jnp.where(value < 0, value + phase_modulus, value)
        return jnp.where(value >= phase_modulus, value - phase_modulus, value)

    lift = (owners * X // phase_modulus + 1) * phase_modulus
    start = modulo(lift + me * X - foot * SPACING - 2 * (C - 1))
    along = lax.broadcasted_iota(jnp.int32, (MOST, chirp), 1)
    turn = turns_of(sums, foot >> 4, foot & (PING_DEV - 1))
    folded = start[:, 0:1] + along
    folded = jnp.where(folded >= phase_modulus, folded - phase_modulus, folded)
    square = modulo(folded * folded)
    phases = square.astype(jnp.float32) * (2.0 * math.pi / phase_modulus) + (
        shift[:, 0:1].astype(jnp.float32) * (math.pi / 4.0) - turn
    )
    cosines[...] = jnp.cos(phases) * scale
    sines[...] = jnp.sin(phases) * scale

    def spread(ref, j):
        return pltpu.roll(
            jnp.broadcast_to(ref[pl.ds(j, 1), :], (C, chirp)),
            chirp - 2 * (C - 1),
            1,
            stride=2,
            stride_axis=0,
        )[:, :X]

    def weigh(pair, carry):
        upper, lower = [], []
        for s in range(2):
            cosine = spread(cosines, 2 * pair + s)
            sine = spread(sines, 2 * pair + s)
            upper += [cosine, -sine]
            lower += [sine, cosine]
        at = pl.ds(pl.multiple_of(pair * 4 * C, 4 * C), 4 * C)
        weights[0:X, at] = jnp.concatenate(upper, axis=0).T.astype(jnp.bfloat16)
        weights[X : 2 * X, at] = jnp.concatenate(lower, axis=0).T.astype(jnp.bfloat16)
        return carry

    lax.fori_loop(0, MOST // 2, weigh, 0)

    for copy in forward[0][2:] + backward[0][2:] + relays[0]:
        copy.wait_recv()

    targets = []
    for k in range(1, HOLD):
        for part in range(2):
            d, dc = k // CORES, k % CORES
            to = device(y + d, x, c + dc) if part == 0 else device(y, x + d, c + dc)
            targets.append((part * HOLD + k, to))
    tiles = length // 128

    def cut(q, part, slot):
        local = table[0, part * HOLD * HOLD + slot]
        offset = table[1, part * HOLD * HOLD + slot]
        back = offset < 0
        rem = jnp.where(back, offset + 128, offset)
        turn = lax.rem(128 - rem, 128)
        keep = lane < 128 - rem
        first = q * wide // 128

        def tile(k):
            if k < 0:
                return jnp.where(use_low, lows[part][local].astype(jnp.float32), 0.0)
            if k >= tiles:
                return jnp.where(use_high, highs[part][local].astype(jnp.float32), 0.0)
            at = 128 * k % span
            return pools[part][128 * k // span][local, :, at : at + 128].astype(jnp.float32)

        here = tile(first)
        current = pltpu.roll(jnp.where(back, tile(first - 1), here), turn, 1)
        out = []
        for k in range(first, first + wide // 128):
            following_tile = tile(k + 1)
            following = pltpu.roll(jnp.where(back, here, following_tile), turn, 1)
            out.append(jnp.where(keep, current, following).astype(jnp.bfloat16))
            current, here = following, following_tile
        return out

    def build(i):
        q = order[i]
        for part in range(2):

            def for_self(s, carry):
                for k, value in enumerate(cut(q, part, s)):
                    received[i][part * HOLD * HOLD + s, :, 128 * k : 128 * (k + 1)] = value
                return carry

            def for_others(s, carry):
                for k, value in enumerate(cut(q, part, s)):
                    staging[i % 2, part * HOLD * HOLD + s, :, 128 * k : 128 * (k + 1)] = value
                return carry

            lax.fori_loop(0, HOLD, for_self, 0, unroll=True)
            lax.fori_loop(HOLD, HOLD * HOLD, for_others, 0, unroll=HOLD)

    def ship(i):
        copies = []
        for k, (group, to) in enumerate(targets):
            at = pl.ds(group * HOLD, HOLD)
            copies.append(
                pltpu.make_async_remote_copy(
                    src_ref=staging.at[i % 2, at],
                    dst_ref=received[i].at[at],
                    send_sem=slot_send.at[i, k],
                    recv_sem=slot_recv.at[i, k],
                    device_id={"ping": to},
                    device_id_type=MESH,
                )
            )
            copies[-1].start()
        return copies

    shipped = []
    for i in range(2):
        build(i)
        shipped.append(ship(i))
    for copy in forward[1][2:] + backward[1][2:] + relays[1]:
        copy.wait_recv()
    for distance in range(1, SIDE):
        send_gathered_edges(distance)
    rows = X
    for i in range(chunks):
        if i + 2 < chunks:
            for copy in shipped[i]:
                copy.wait_send()
            if i + 2 == order.index(0):
                for copy in edge_copies:
                    copy.wait_recv()
            build(i + 2)
            shipped.append(ship(i + 2))
        for copy in shipped[i]:
            copy.wait_recv()

        def fill(j, carry):
            for part in range(2):
                at = pl.multiple_of(j * 2 * C + part * C, C)
                stacked[pl.ds(at, C), :] = received[i][arrival[part, j]]
            return carry

        lax.fori_loop(0, MOST, fill, 0, unroll=8)
        before[i].wait()

        def multiply(k, carry):
            at = pl.ds(pl.multiple_of(k * rows, rows), rows)
            product = jnp.dot(weights[at, :], stacked[...], preferred_element_type=jnp.float32)
            image[i % 2, at, :] = (image[i % 2, at, :].astype(jnp.float32) + product).astype(
                jnp.bfloat16
            )
            return carry

        lax.fori_loop(0, 2 * X // rows, multiply, 0)
        after[i].start()
        if i >= 1 and i + 1 < chunks:
            after[i - 1].wait()
            before[i + 1].start()
    for copy in started + across + edge_copies + spread_sums + shipped[chunks - 2] + shipped[chunks - 1]:
        copy.wait_send()
    for copy in after[chunks - 2 :]:
        copy.wait()


def focus(footprint, counts, offsets, pairing, echoes, earlier, rng_size):
    pings, parts, channels, length = echoes.shape
    owners = SIDE * SIDE * CORES
    chunks = 8
    wide = length // chunks
    slots = 2 * HOLD * HOLD
    count = 2 * (HOLD - 1)
    bf16, f32 = jnp.bfloat16, jnp.float32
    dma = pltpu.SemaphoreType.DMA
    steps = 1 + 16 + 8
    smem = pl.BlockSpec(memory_space=pltpu.SMEM)
    return pl.pallas_call(
        functools.partial(image_kernel, rng_size),
        out_shape=jax.ShapeDtypeStruct((2 * X, length), bf16),
        in_specs=[smem] * 4 + [ANY, ANY],
        out_specs=ANY,
        scratch_shapes=[
            pltpu.SMEM((2, slots), jnp.int32),
            pltpu.SMEM((2, MOST), jnp.int32),
            *[pltpu.VMEM((SIDE * pings, channels, length // 2), bf16)] * 4,
            *[pltpu.VMEM((SIDE * pings, channels, 128), bf16)] * 4,
            pltpu.VMEM((parts, channels, length), bf16),
            pltpu.VMEM((rng_size, 1, 128), f32),
            pltpu.VMEM((1, 128), f32),
            pltpu.VMEM((owners, 1, 128), f32),
            pltpu.VMEM((2, slots, channels, wide), bf16),
            pltpu.VMEM((2 * X, MOST * 2 * C), bf16),
            pltpu.VMEM((MOST * 2 * C, wide), bf16),
            pltpu.VMEM((2, 2 * X, wide), bf16),
            pltpu.VMEM((MOST, X + 128), f32),
            pltpu.VMEM((MOST, X + 128), f32),
            dma((4 + 2 * chunks,)),
            dma((steps,)),
            dma((steps,)),
            dma((owners + rng_size,)),
            dma((owners + rng_size,)),
            dma((chunks, count)),
            dma((chunks, count)),
            dma((4 * SIDE,)),
            dma((4 * SIDE,)),
        ]
        + [pltpu.VMEM((slots, channels, wide), bf16)] * chunks,
        compiler_params=pltpu.CompilerParams(
            collective_id=0, has_side_effects=True, vmem_limit_bytes=63 << 20
        ),
        name="focus",
    )(footprint, counts, offsets, pairing, echoes, earlier)


def move_kernel(source, target, held, load_sem, store_sem):
    pieces = load_sem.shape[0]
    rows = held.shape[0] // pieces
    loads, stores = [], []
    for i in range(pieces):
        at = pl.ds(rows * i, rows)
        loads.append(pltpu.make_async_copy(source.at[at], held.at[at], load_sem.at[i]))
        stores.append(pltpu.make_async_copy(held.at[at], target.at[at], store_sem.at[i]))
        loads[-1].start()
    for load, store in zip(loads, stores):
        load.wait()
        store.start()
    for store in stores:
        store.wait()


def move(image):
    return pl.pallas_call(
        move_kernel,
        out_shape=jax.ShapeDtypeStruct(image.shape, image.dtype),
        in_specs=[ANY],
        out_specs=ANY,
        scratch_shapes=[
            pltpu.VMEM(image.shape, image.dtype),
            pltpu.SemaphoreType.DMA((8,)),
            pltpu.SemaphoreType.DMA((8,)),
        ],
        name="move",
    )(image)


def per_device(echoes, pairing, footprint, counts, offsets, earlier):
    rng_size = lax.axis_size("rng")
    image = focus(
        footprint,
        counts,
        offsets,
        pairing,
        echoes,
        earlier.reshape(2 * X, echoes.shape[3]),
        rng_size,
    )
    return move(image).reshape(earlier.shape)


def solution(mesh):
    return jax.shard_map(
        per_device,
        mesh=mesh,
        in_specs=(
            P("ping", None, None, "rng"),
            P("ping", None, None),
            P(),
            P(),
            P(),
            P("ping", None, None, "rng"),
        ),
        out_specs=P("ping", None, None, "rng"),
        check_vma=False,
    )
```

```python
import functools
import math

import jax
import jax.numpy as jnp
from jax import lax
from jax.experimental import pallas as pl
from jax.experimental.pallas import tpu as pltpu
from jax.sharding import PartitionSpec as P

C = 32
X = 1024
MOST = 48
PING_DEV = 16
SPACING = X // PING_DEV
SIDE = 4
CORES = 2
HOLD = 8
MESH = pl.DeviceIdType.MESH
ANY = pl.BlockSpec(memory_space=pl.ANY)

phase_modulus = 4099
small_value = 1e-06


def place(index):
    return index // (SIDE * CORES), (index // CORES) % SIDE, index % CORES


def device(y, x, c):
    return (((y + SIDE) % SIDE) * SIDE + (x + SIDE) % SIDE) * CORES + (c + CORES) % CORES


def turns_of(sums_ref, owner, local):
    sums = sums_ref[:, 0, :]
    owners = sums.shape[0]
    lane = lax.broadcasted_iota(jnp.int32, (owners, 128), 1)
    row = lax.broadcasted_iota(jnp.int32, (owners, 128), 0)
    front = pltpu.roll(sums, 128 - PING_DEV, 1)
    rear = pltpu.roll(sums, 128 - 2 * PING_DEV, 1)
    valid = lane < PING_DEV
    energy = jnp.where(valid, front * rear, 1.0)
    running = jnp.where(valid, sums / (jnp.sqrt(energy) + small_value), 0.0)
    step = 1
    while step < PING_DEV:
        running = running + jnp.where(lane >= step, pltpu.roll(running, step, 1), 0.0)
        step *= 2
    last = jnp.sum(jnp.where(lane == PING_DEV - 1, running, 0.0), axis=1, keepdims=True)
    before = jnp.broadcast_to(last, (owners, 128))
    step = 1
    while step < owners:
        before = before + jnp.where(row >= step, pltpu.roll(before, step, 0), 0.0)
        step *= 2
    before = jnp.where(row >= 1, pltpu.roll(before, 1, 0), 0.0)
    turn = jnp.where(valid, running + before, 0.0)
    entries = owner.shape[0]
    lane = lax.broadcasted_iota(jnp.int32, (entries, 128), 1)
    at_lane = lane == local
    picked = jnp.zeros((entries, 128), jnp.float32)
    for k in range(owners):
        picked = picked + jnp.where(at_lane & (owner == k), turn[k : k + 1, :], 0.0)
    return jnp.sum(picked, axis=1, keepdims=True)


def image_kernel(
    rng_size,
    footprint,
    counts,
    offsets,
    pairing,
    echo_ref,
    earlier_ref,
    out_ref,
    table,
    arrival,
    row_first,
    row_second,
    column_first,
    column_second,
    row_low,
    row_high,
    column_low,
    column_high,
    lead,
    partial,
    total,
    sums,
    staging,
    weights,
    stacked,
    image,
    cosines,
    sines,
    local_sem,
    send_sem,
    recv_sem,
    sum_send,
    sum_recv,
    slot_send,
    slot_recv,
    edge_send,
    edge_recv,
    *received,
):
    me = lax.axis_index("ping")
    level = lax.axis_index("rng")
    y, x, c = place(me)
    owners = SIDE * SIDE * CORES
    pings, half = PING_DEV, PING_DEV // 2
    length = echo_ref.shape[3]
    chunks, wide = len(received), stacked.shape[1]
    order = [1, 2, 4, 5, 6, 3, 0, 7]

    barrier = pltpu.get_barrier_semaphore()
    for step in range(1, owners):
        pl.semaphore_signal(
            barrier, inc=1, device_id={"ping": (me + step) % owners}, device_id_type=MESH
        )
    for step in range(1, rng_size):
        pl.semaphore_signal(
            barrier, inc=1, device_id={"rng": (level + step) % rng_size}, device_id_type=MESH
        )
    pools = ((row_first, row_second), (column_first, column_second))
    lows, highs = (row_low, column_low), (row_high, column_high)
    span = length // 2
    spans = (pl.ds(0, span), pl.ds(span, span))
    own = [
        pltpu.make_async_copy(
            echo_ref.at[:, part, :, spans[h]],
            pools[part][h].at[pl.ds(0, pings)],
            local_sem.at[2 * chunks + 2 * part + h],
        )
        for part in range(2)
        for h in range(2)
    ]
    before = [
        pltpu.make_async_copy(
            earlier_ref.at[:, pl.ds(order[q] * wide, wide)], image.at[q % 2], local_sem.at[q]
        )
        for q in range(chunks)
    ]
    after = [
        pltpu.make_async_copy(
            image.at[q % 2], out_ref.at[:, pl.ds(order[q] * wide, wide)], local_sem.at[chunks + q]
        )
        for q in range(chunks)
    ]
    for copy in own + before[:2]:
        copy.start()
    pl.semaphore_wait(barrier, owners + rng_size - 2)

    started = []

    def send(src, dst, target):
        i = len(started)
        copy = pltpu.make_async_remote_copy(
            src_ref=src,
            dst_ref=dst,
            send_sem=send_sem.at[i],
            recv_sem=recv_sem.at[i],
            device_id=target,
            device_id_type=MESH,
        )
        copy.start()
        started.append(copy)
        return copy

    up, down = {"rng": (level + 1) % rng_size}, {"rng": (level + rng_size - 1) % rng_size}
    ahead = {"ping": device(y, x + 1, c)}
    behind = {"ping": device(y, x - 1, c)}
    above = {"ping": device(y + 1, x, c)}
    below = {"ping": device(y - 1, x, c)}
    from_lead = send(echo_ref.at[pings - 1], lead, {"ping": (me + 1) % owners})

    edge_copies = []

    def send_edges(sources_low, sources_high, at):
        for part in range(2):
            for source, pool, target in (
                (sources_low[part], lows[part], up),
                (sources_high[part], highs[part], down),
            ):
                i = len(edge_copies)
                edge_copies.append(
                    pltpu.make_async_remote_copy(
                        src_ref=source,
                        dst_ref=pool.at[at],
                        send_sem=edge_send.at[i],
                        recv_sem=edge_recv.at[i],
                        device_id=target,
                        device_id_type=MESH,
                    )
                )
                edge_copies[-1].start()

    def send_gathered_edges(distance):
        at = pl.ds(distance * pings, pings)
        send_edges(
            [pools[part][1].at[at, :, pl.ds(span - 128, 128)] for part in range(2)],
            [pools[part][0].at[at, :, pl.ds(0, 128)] for part in range(2)],
            at,
        )

    send_edges(
        [echo_ref.at[:, part, :, pl.ds(length - 128, 128)] for part in range(2)],
        [echo_ref.at[:, part, :, pl.ds(0, 128)] for part in range(2)],
        pl.ds(0, pings),
    )
    ways = ((0, ahead, behind), (1, above, below))
    pieces = [
        [((0, m), (m, pings - m)) for m in ((half - 1, half) if part == 0 else (half, half))]
        for part in range(2)
    ]
    forward, backward = [[], []], [[], []]
    for h in range(2):
        for turn in range(2):
            for part, forth, back in ways:
                pool = pools[part][h]
                at, size = pieces[part][h][turn]
                forward[h].append(
                    send(
                        echo_ref.at[pl.ds(at, size), part, :, spans[h]],
                        pool.at[pl.ds(3 * pings + at, size)],
                        forth,
                    )
                )
                at, size = pieces[part][h][1 - turn]
                backward[h].append(
                    send(
                        echo_ref.at[pl.ds(at, size), part, :, spans[h]],
                        pool.at[pl.ds(pings + at, size)],
                        back,
                    )
                )

    lane = lax.broadcasted_iota(jnp.int32, (C, 128), 1)
    use_low = level > 0
    use_high = level < rng_size - 1

    def owner_of(ping):
        owner = ping >> 4
        return owner >> 3, (owner >> 1) & (SIDE - 1), owner & (CORES - 1)

    for part in range(2):
        for k in range(HOLD):
            d, dc = k // CORES, k % CORES
            tile_id = device(y + d, x, c + dc) if part == 0 else device(y, x + d, c + dc)
            limit = counts[tile_id]

            def scan(j, carry, part=part, tile_id=tile_id, limit=limit):
                filled, sources, shifts = carry
                ping = footprint[tile_id, j]
                oy, ox, oc = owner_of(ping)
                near = oy == y if part == 0 else ox == x
                match = near & (oc == c) & (j < limit)
                away = (ox - x if part == 0 else oy - y) + SIDE
                source = (away & (SIDE - 1)) * PING_DEV + (ping & (PING_DEV - 1))
                shift = offsets[tile_id, j]
                at = jnp.where(match, filled, -1)
                sources = tuple(jnp.where(at == i, source, v) for i, v in enumerate(sources))
                shifts = tuple(jnp.where(at == i, shift, v) for i, v in enumerate(shifts))
                return filled + match.astype(jnp.int32), sources, shifts

            zeros = (jnp.int32(0),) * HOLD
            _, sources, shifts = lax.fori_loop(0, MOST, scan, (jnp.int32(0), zeros, zeros))
            for i in range(HOLD):
                table[0, (part * HOLD + k) * HOLD + i] = sources[i]
                table[1, (part * HOLD + k) * HOLD + i] = shifts[i]

    own_limit = counts[me]
    for part in range(2):

        def scan_own(j, carry, part=part):
            first, held = carry
            oy, ox, oc = owner_of(footprint[me, j])
            at = oy if part == 0 else ox
            group = at * CORES + oc
            rank = jnp.int32(0)
            for g in range(HOLD):
                rank = jnp.where(group == g, held[g], rank)
            away = ((y if part == 0 else x) - at + SIDE) & (SIDE - 1)
            core = (c - oc + CORES) & (CORES - 1)
            slot = ((part * SIDE + away) * CORES + core) * HOLD + rank
            first = jnp.where(j == 0, slot, first)
            listed = j < own_limit
            arrival[part, j] = jnp.where(listed, slot, first)
            entered = jnp.where(listed, group, -1)
            held = tuple(v + jnp.where(entered == g, 1, 0) for g, v in enumerate(held))
            return first, held

        lax.fori_loop(0, MOST, scan_own, (jnp.int32(0), (jnp.int32(0),) * HOLD))

    for copy in own:
        copy.wait()
    from_lead.wait_recv()
    place_lane = lax.broadcasted_iota(jnp.int32, (1, 128), 1)

    def fold(value):
        out = value[:, 0:128]
        for k in range(1, span // 128):
            out = out + value[:, 128 * k : 128 * (k + 1)]
        out = jnp.sum(out, axis=0, keepdims=True)
        return jnp.sum(out, axis=1, keepdims=True)

    pair_row = lax.broadcasted_iota(jnp.int32, (8, C), 0)
    channel = lax.broadcasted_iota(jnp.int32, (8, C), 1)

    def picks(p, side):
        wanted = jnp.zeros((8, C), jnp.int32)
        for k in range(8):
            wanted = jnp.where(pair_row == k, pairing[p, side, k], wanted)
        return jnp.where(channel == wanted, 1.0, 0.0).astype(jnp.bfloat16)

    def correlate(p, front_source, acc):
        front, rear = picks(p, 0), picks(p, 1)
        dot = functools.partial(jnp.dot, preferred_element_type=jnp.float32)
        cross = front_energy = rear_energy = 0.0
        for h in range(2):
            front_real = dot(front, front_source(0, h))
            front_imag = dot(front, front_source(1, h))
            rear_real = dot(rear, pools[0][h][p])
            rear_imag = dot(rear, pools[1][h][p])
            cross = cross + fold(front_real * rear_imag - front_imag * rear_real)
            front_energy = front_energy + fold(front_real * front_real + front_imag * front_imag)
            rear_energy = rear_energy + fold(rear_real * rear_real + rear_imag * rear_imag)
        acc = jnp.where(place_lane == p, cross, acc)
        acc = jnp.where(place_lane == p + pings, front_energy, acc)
        return jnp.where(place_lane == p + 2 * pings, rear_energy, acc)

    mine = correlate(
        0, lambda part, h: lead[part, :, span * h : span * (h + 1)], jnp.zeros((1, 128), jnp.float32)
    )
    mine = jnp.where((me == 0) & (place_lane < 2 * pings), 0.0, mine)
    mine = lax.fori_loop(
        1, pings, lambda p, acc: correlate(p, lambda part, h: pools[part][h][p - 1], acc), mine
    )
    partial[0] = mine

    across = []
    for step in range(1, rng_size):
        across.append(
            pltpu.make_async_remote_copy(
                src_ref=partial.at[0],
                dst_ref=partial.at[step],
                send_sem=sum_send.at[owners + step],
                recv_sem=sum_recv.at[owners + step],
                device_id={"rng": (level + step) % rng_size},
                device_id_type=MESH,
            )
        )
        across[-1].start()
    for copy in across:
        copy.wait_recv()
    whole = mine
    for step in range(1, rng_size):
        whole = whole + partial[step]
    total[...] = whole
    sums[me] = whole
    spread_sums = []
    for step in range(1, owners):
        spread_sums.append(
            pltpu.make_async_remote_copy(
                src_ref=total,
                dst_ref=sums.at[me],
                send_sem=sum_send.at[step],
                recv_sem=sum_recv.at[step],
                device_id={"ping": (me + step) % owners},
                device_id_type=MESH,
            )
        )
        spread_sums[-1].start()

    relays = [[], []]
    for h in range(2):
        for part, forth, back in ways:
            pool = pools[part][h]
            (at, size), (later, rest) = pieces[part][h]
            forward[h][part].wait_recv()
            source, target = pl.ds(3 * pings + at, size), pl.ds(2 * pings + at, size)
            relays[h].append(send(pool.at[source], pool.at[target], forth))
            backward[h][part].wait_recv()
            source, target = pl.ds(pings + later, rest), pl.ds(2 * pings + later, rest)
            relays[h].append(send(pool.at[source], pool.at[target], back))
    for copy in spread_sums:
        copy.wait_recv()

    chirp = cosines.shape[1]
    entry = lax.broadcasted_iota(jnp.int32, (MOST, 128), 0)
    foot = jnp.zeros((MOST, 128), jnp.int32)
    shift = jnp.zeros((MOST, 128), jnp.int32)
    for j in range(MOST):
        foot = jnp.where(entry == j, footprint[me, j], foot)
        shift = jnp.where(entry == j, offsets[me, j], shift)
    listed = jnp.where(entry < own_limit, 1.0, 0.0)
    channels = jnp.full((MOST, 128), own_limit, jnp.int32).astype(jnp.float32) * jnp.float32(C)
    scale = (listed / jnp.sqrt(channels))[:, 0:1]

    def modulo(value):
        value = value - phase_modulus * (
            value.astype(jnp.float32) * (1.0 / phase_modulus)
        ).astype(jnp.int32)
        value = jnp.where(value < 0, value + phase_modulus, value)
        return jnp.where(value >= phase_modulus, value - phase_modulus, value)

    lift = (owners * X // phase_modulus + 1) * phase_modulus
    start = modulo(lift + me * X - foot * SPACING - 2 * (C - 1))
    along = lax.broadcasted_iota(jnp.int32, (MOST, chirp), 1)
    turn = turns_of(sums, foot >> 4, foot & (PING_DEV - 1))
    folded = start[:, 0:1] + along
    folded = jnp.where(folded >= phase_modulus, folded - phase_modulus, folded)
    square = modulo(folded * folded)
    phases = square.astype(jnp.float32) * (2.0 * math.pi / phase_modulus) + (
        shift[:, 0:1].astype(jnp.float32) * (math.pi / 4.0) - turn
    )
    cosines[...] = jnp.cos(phases) * scale
    sines[...] = jnp.sin(phases) * scale

    def spread(ref, j):
        return pltpu.roll(
            jnp.broadcast_to(ref[pl.ds(j, 1), :], (C, chirp)),
            chirp - 2 * (C - 1),
            1,
            stride=2,
            stride_axis=0,
        )[:, :X]

    def weigh(pair, carry):
        upper, lower = [], []
        for s in range(2):
            cosine = spread(cosines, 2 * pair + s)
            sine = spread(sines, 2 * pair + s)
            upper += [cosine, -sine]
            lower += [sine, cosine]
        at = pl.ds(pl.multiple_of(pair * 4 * C, 4 * C), 4 * C)
        weights[0:X, at] = jnp.concatenate(upper, axis=0).T.astype(jnp.bfloat16)
        weights[X : 2 * X, at] = jnp.concatenate(lower, axis=0).T.astype(jnp.bfloat16)
        return carry

    lax.fori_loop(0, MOST // 2, weigh, 0)

    for copy in forward[0][2:] + backward[0][2:] + relays[0]:
        copy.wait_recv()

    targets = []
    for k in range(1, HOLD):
        for part in range(2):
            d, dc = k // CORES, k % CORES
            to = device(y + d, x, c + dc) if part == 0 else device(y, x + d, c + dc)
            targets.append((part * HOLD + k, to))
    tiles = length // 128

    def cut(q, part, slot):
        local = table[0, part * HOLD * HOLD + slot]
        offset = table[1, part * HOLD * HOLD + slot]
        back = offset < 0
        rem = jnp.where(back, offset + 128, offset)
        turn = lax.rem(128 - rem, 128)
        keep = lane < 128 - rem
        first = q * wide // 128

        def tile(k):
            if k < 0:
                return jnp.where(use_low, lows[part][local].astype(jnp.float32), 0.0)
            if k >= tiles:
                return jnp.where(use_high, highs[part][local].astype(jnp.float32), 0.0)
            at = 128 * k % span
            return pools[part][128 * k // span][local, :, at : at + 128].astype(jnp.float32)

        here = tile(first)
        current = pltpu.roll(jnp.where(back, tile(first - 1), here), turn, 1)
        out = []
        for k in range(first, first + wide // 128):
            following_tile = tile(k + 1)
            following = pltpu.roll(jnp.where(back, here, following_tile), turn, 1)
            out.append(jnp.where(keep, current, following).astype(jnp.bfloat16))
            current, here = following, following_tile
        return out

    def build(i):
        q = order[i]
        for part in range(2):

            def for_self(s, carry):
                for k, value in enumerate(cut(q, part, s)):
                    received[i][part * HOLD * HOLD + s, :, 128 * k : 128 * (k + 1)] = value
                return carry

            def for_others(s, carry):
                for k, value in enumerate(cut(q, part, s)):
                    staging[i % 2, part * HOLD * HOLD + s, :, 128 * k : 128 * (k + 1)] = value
                return carry

            lax.fori_loop(0, HOLD, for_self, 0, unroll=True)
            lax.fori_loop(HOLD, HOLD * HOLD, for_others, 0, unroll=HOLD)

    def ship(i):
        copies = []
        for k, (group, to) in enumerate(targets):
            at = pl.ds(group * HOLD, HOLD)
            copies.append(
                pltpu.make_async_remote_copy(
                    src_ref=staging.at[i % 2, at],
                    dst_ref=received[i].at[at],
                    send_sem=slot_send.at[i, k],
                    recv_sem=slot_recv.at[i, k],
                    device_id={"ping": to},
                    device_id_type=MESH,
                )
            )
            copies[-1].start()
        return copies

    shipped = []
    for i in range(2):
        build(i)
        shipped.append(ship(i))
    for copy in forward[1][2:] + backward[1][2:] + relays[1]:
        copy.wait_recv()
    for distance in range(1, SIDE):
        send_gathered_edges(distance)
    rows = X
    for i in range(chunks):
        if i + 2 < chunks:
            for copy in shipped[i]:
                copy.wait_send()
            if i + 2 == order.index(0):
                for copy in edge_copies:
                    copy.wait_recv()
            build(i + 2)
            shipped.append(ship(i + 2))
        for copy in shipped[i]:
            copy.wait_recv()

        def fill(j, carry):
            for part in range(2):
                at = pl.multiple_of(j * 2 * C + part * C, C)
                stacked[pl.ds(at, C), :] = received[i][arrival[part, j]]
            return carry

        lax.fori_loop(0, MOST, fill, 0, unroll=8)
        before[i].wait()

        def multiply(k, carry):
            at = pl.ds(pl.multiple_of(k * rows, rows), rows)
            product = jnp.dot(weights[at, :], stacked[...], preferred_element_type=jnp.float32)
            image[i % 2, at, :] = (image[i % 2, at, :].astype(jnp.float32) + product).astype(
                jnp.bfloat16
            )
            return carry

        lax.fori_loop(0, 2 * X // rows, multiply, 0)
        after[i].start()
        if i >= 1 and i + 1 < chunks:
            after[i - 1].wait()
            before[i + 1].start()
    for copy in started + across + edge_copies + spread_sums + shipped[chunks - 2] + shipped[chunks - 1]:
        copy.wait_send()
    for copy in after[chunks - 2 :]:
        copy.wait()


def focus(footprint, counts, offsets, pairing, echoes, earlier, rng_size):
    pings, parts, channels, length = echoes.shape
    owners = SIDE * SIDE * CORES
    chunks = 8
    wide = length // chunks
    slots = 2 * HOLD * HOLD
    count = 2 * (HOLD - 1)
    bf16, f32 = jnp.bfloat16, jnp.float32
    dma = pltpu.SemaphoreType.DMA
    steps = 1 + 16 + 8
    smem = pl.BlockSpec(memory_space=pltpu.SMEM)
    return pl.pallas_call(
        functools.partial(image_kernel, rng_size),
        out_shape=jax.ShapeDtypeStruct((2 * X, length), bf16),
        in_specs=[smem] * 4 + [ANY, ANY],
        out_specs=ANY,
        scratch_shapes=[
            pltpu.SMEM((2, slots), jnp.int32),
            pltpu.SMEM((2, MOST), jnp.int32),
            *[pltpu.VMEM((SIDE * pings, channels, length // 2), bf16)] * 4,
            *[pltpu.VMEM((SIDE * pings, channels, 128), bf16)] * 4,
            pltpu.VMEM((parts, channels, length), bf16),
            pltpu.VMEM((rng_size, 1, 128), f32),
            pltpu.VMEM((1, 128), f32),
            pltpu.VMEM((owners, 1, 128), f32),
            pltpu.VMEM((2, slots, channels, wide), bf16),
            pltpu.VMEM((2 * X, MOST * 2 * C), bf16),
            pltpu.VMEM((MOST * 2 * C, wide), bf16),
            pltpu.VMEM((2, 2 * X, wide), bf16),
            pltpu.VMEM((MOST, X + 128), f32),
            pltpu.VMEM((MOST, X + 128), f32),
            dma((4 + 2 * chunks,)),
            dma((steps,)),
            dma((steps,)),
            dma((owners + rng_size,)),
            dma((owners + rng_size,)),
            dma((chunks, count)),
            dma((chunks, count)),
            dma((4 * SIDE,)),
            dma((4 * SIDE,)),
        ]
        + [pltpu.VMEM((slots, channels, wide), bf16)] * chunks,
        compiler_params=pltpu.CompilerParams(
            collective_id=0, has_side_effects=True, vmem_limit_bytes=63 << 20
        ),
        name="focus",
    )(footprint, counts, offsets, pairing, echoes, earlier)


def move_kernel(source, target, held, load_sem, store_sem):
    pieces = load_sem.shape[0]
    rows = held.shape[0] // pieces
    loads, stores = [], []
    for i in range(pieces):
        at = pl.ds(rows * i, rows)
        loads.append(pltpu.make_async_copy(source.at[at], held.at[at], load_sem.at[i]))
        stores.append(pltpu.make_async_copy(held.at[at], target.at[at], store_sem.at[i]))
        loads[-1].start()
    for load, store in zip(loads, stores):
        load.wait()
        store.start()
    for store in stores:
        store.wait()


def move(image):
    return pl.pallas_call(
        move_kernel,
        out_shape=jax.ShapeDtypeStruct(image.shape, image.dtype),
        in_specs=[ANY],
        out_specs=ANY,
        scratch_shapes=[
            pltpu.VMEM(image.shape, image.dtype),
            pltpu.SemaphoreType.DMA((8,)),
            pltpu.SemaphoreType.DMA((8,)),
        ],
        name="move",
    )(image)


def per_device(echoes, pairing, footprint, counts, offsets, earlier):
    rng_size = lax.axis_size("rng")
    image = focus(
        footprint,
        counts,
        offsets,
        pairing,
        echoes,
        earlier.reshape(2 * X, echoes.shape[3]),
        rng_size,
    )
    return move(image).reshape(earlier.shape)


def solution(mesh):
    return jax.shard_map(
        per_device,
        mesh=mesh,
        in_specs=(
            P("ping", None, None, "rng"),
            P("ping", None, None),
            P(),
            P(),
            P(),
            P("ping", None, None, "rng"),
        ),
        out_specs=P("ping", None, None, "rng"),
        check_vma=False,
    )
```
